32 devices in a mesh: dp: 4 (over y, x), expert: 8 (over z, core).
Axes of the slice: x: 2, y: 2, z: 4, core: 2. Of those that a mesh axis runs over, the one named last changes fastest.
Arguments:
- tokens: bfloat16 [4096, 2048], P(('dp', 'expert')), may hold values from -70 to 70
- routing: int32 [4096, 2], P(('dp', 'expert')), may hold values from 0 to 7, all different within a row; in each aligned block of 128 rows (0 to 127, 128 to 255, ...) at most 40 rows name the same one
- probs: bfloat16 [4096, 2], P(('dp', 'expert')), may hold values from 0.099609375 to 1
- cotangent: bfloat16 [4096, 2048], P(('dp', 'expert')), may hold values from -70 to 70
- w_gate: bfloat16 [8, 2048, 512], P('expert'), may hold values from -0.125 to 0.125
- w_up: bfloat16 [8, 2048, 512], P('expert'), may hold values from -0.125 to 0.125
- w_down: bfloat16 [8, 512, 2048], P('expert'), may hold values from -0.25 to 0.25
Outputs:
- grad_gate: float32 [8, 2048, 512], P('expert', 'dp')
- grad_up: float32 [8, 2048, 512], P('expert', 'dp')
- grad_down: float32 [8, 512, 2048], P('expert', None, 'dp')
- input_grad: bfloat16 [4096, 2048], P(('dp', 'expert'))
- router_grad: bfloat16 [4096, 2], P(('dp', 'expert'))
The draws below stay inside these ranges and needn't reach their ends.
Inputs may be any that keep to these rules, and one draw needn't show every extreme that they name: `routing`: each row names 2 different experts. Among the 128 rows of one device no expert is named more than 40 times, a bound that some block reaches.
All inputs are finite; a program needn't handle non-finite values.
Results may differ from the reference program's by a relative error of at most 0.0065.
Values may be sent and summed in bfloat16 or wider, within the bound.
A program may use at most 64 MiB of HBM per device.

```python
import math
import jax
import jax.numpy as jnp
import numpy as np
from jax import lax

D = 2048
FF = 512
TOK_DEV = 128
TOP = 2
EXPERTS = 8
CAP = 40
TOKENS = 4096
LEVELS = 2
N_DP = 4
N_EXPERT = 8


def shifted_rows(key, salt_value, row_count, col_count):
    first_key, second_key = jax.random.split(jax.random.fold_in(key, salt_value), 2)
    column = jnp.arange(col_count, dtype=jnp.float32) / (col_count - 1)
    spread = 10.0 ** column / 3.0
    shared = jnp.clip(jax.random.normal(first_key, (col_count,), jnp.float32), -3.0, 3.0)
    jitter = jnp.clip(jax.random.normal(second_key, (row_count, col_count), jnp.float32), -4.0, 4.0)
    values = 0.6 * shared[None, :] + jitter
    return (values * spread[None, :]).astype(jnp.bfloat16)


def draw_tokens(key, part):
    return shifted_rows(key, 11, TOKENS, D)


def draw_cotangent(key, part):
    return shifted_rows(key, 23, TOKENS, D)


def levels(own_key, extent, pieces, smallest, largest):
    factor_of = 1.0
    for dim, blocks in pieces:
        heights = jax.random.uniform(jax.random.fold_in(jax.random.fold_in(own_key, 6), dim), (blocks,), jnp.float32, smallest / len(pieces), largest / len(pieces))
        factor_of = factor_of * jnp.repeat(jnp.exp(heights), extent[dim] // blocks).reshape((-1,) + (1,) * (len(extent) - 1 - dim))
    return factor_of


def deal_out(key, own, number, rows, amount, top, bound, slope):
    ranking = jax.random.permutation(key, amount)
    packed, ordinary = load_shares(amount, rows * top, bound, slope, True), load_shares(amount, rows * top, bound, slope, False)
    places = jnp.arange(amount)

    def named(sizes, turn):
        used = int((sizes > 0).sum())
        fixed = max(1, used // 4)
        passed = fixed + (places - fixed + turn * (used - fixed)) % max(1, amount - fixed)
        return jnp.zeros((amount,), jnp.int32).at[ranking[jnp.where(places < fixed, places, passed)]].set(jnp.asarray(sizes, jnp.int32))

    sizes = jnp.where(number % 4 == 0, named(packed, number // 4), named(ordinary, number - number // 4 - 1))
    mixed = jax.random.permutation(jax.random.fold_in(own, 3), amount)
    source_of, sink = mixed[0:amount // 2 * 2:2], mixed[1:amount // 2 * 2:2]
    room = jnp.minimum(sizes[source_of] - 1, bound - sizes[sink]) // 2
    room = jnp.where((source_of == ranking[0]) | (sink == ranking[0]) | (sizes[sink] == 0), 0, jnp.maximum(room, 0))
    passed = jax.random.randint(jax.random.fold_in(own, 4), (amount // 2,), 0, 1 << 20) % (room + 1)
    sizes = sizes.at[source_of].add(-passed).at[sink].add(passed)
    labels = jnp.searchsorted(jnp.cumsum(sizes), jnp.arange(rows * top), side="right").astype(jnp.int32)
    listing = labels.reshape(top, rows).T
    listing = listing[jax.random.permutation(jax.random.fold_in(own, 1), rows)]
    turn = jax.random.randint(jax.random.fold_in(own, 2), (rows, 1), 0, top)
    return jnp.take_along_axis(listing, (jnp.arange(top)[None, :] + turn) % top, axis=1)


def load_shares(count, total, most, skew, full):
    portions = [(1 << 20) // math.isqrt(standing ** skew) + 1 for standing in range(1, count + 1)]
    largest = most if full else min(most, max(-(-total // count), total * portions[0] // sum(portions)))
    least = 1 if total - largest >= count - 1 else 0
    holding, spare = [largest] + [least] * (count - 1), total - largest - least * (count - 1)
    while spare > 0:
        free = [i for i in range(1, count) if holding[i] < largest] or [i for i in range(1, count) if holding[i] < most]
        pool, budget = sum([portions[i] for i in free]), spare
        for i in free:
            extra = min(most - holding[i], max(1, budget * portions[i] // pool), spare)
            holding[i] = holding[i] + extra
            spare = spare - extra
    return np.array(holding)


def normal_values(rng, dims, scale, reach, cuts=(), held_as=jnp.bfloat16):
    entries = jax.random.normal(rng, dims, jnp.float32) * scale
    if len(cuts) > 0:
        entries = levels(rng, dims, cuts, -0.22, 0.18) * entries
    return jnp.clip(entries, min=-reach, max=reach).astype(held_as)


def setup_inputs(seed: int = 0) -> dict:
    arg_keys = jax.random.split(jax.random.key(seed), 8)
    tokens = draw_tokens(jax.random.fold_in(arg_keys[7], 71), 0)
    routing_keys = jax.random.split(jax.random.fold_in(arg_keys[1], 1), TOKENS // TOK_DEV)
    routing_turns = jax.random.permutation(jax.random.fold_in(arg_keys[1], 3), TOKENS // TOK_DEV)
    routing = jax.vmap(lambda own, number: deal_out(jax.random.fold_in(arg_keys[1], 2), own, number, TOK_DEV, EXPERTS, TOP, CAP, 2))(routing_keys, routing_turns).reshape((TOKENS, TOP))
    probs = jnp.clip(0.099609375 + 0.9003906 * jax.random.uniform(arg_keys[2], (TOKENS, TOP), jnp.float32) ** levels(arg_keys[2], (TOKENS, TOP), ((0, 32),), -0.2, 0.2), 0.099609375, 1.0).astype(jnp.bfloat16)
    cotangent = draw_cotangent(jax.random.fold_in(arg_keys[7], 71), 0)
    w_gate = normal_values(arg_keys[4], (EXPERTS, D, FF), D ** -0.5, 0.125, ((0, 8),))
    w_up = normal_values(arg_keys[5], (EXPERTS, D, FF), D ** -0.5, 0.125, ((0, 8),))
    w_down = normal_values(arg_keys[6], (EXPERTS, FF, D), FF ** -0.5, 0.25, ((0, 8),))
    return {"tokens": tokens, "routing": routing, "probs": probs, "cotangent": cotangent, "w_gate": w_gate, "w_up": w_up, "w_down": w_down}


epsilon = 1e-6


def slot_index(routing_block):
    flattened = routing_block.reshape(-1)
    onehot = (flattened[:, None] == jnp.arange(EXPERTS, dtype=jnp.int32)[None, :]).astype(jnp.int32)
    before = jnp.cumsum(onehot, axis=0) - onehot
    return (flattened * CAP + jnp.sum(before * onehot, axis=1)).astype(jnp.int32)


def expert_pass(routed, cot_rows, prob_rows, gate_matrix, up_matrix, down_matrix):
    gate_pre = jnp.dot(routed, gate_matrix, preferred_element_type=jnp.float32)
    up_pre = jnp.dot(routed, up_matrix, preferred_element_type=jnp.float32)
    sigmoid = jax.nn.sigmoid(gate_pre)
    activated = gate_pre * sigmoid
    hidden = (activated * up_pre).astype(jnp.bfloat16)
    output = jnp.dot(hidden, down_matrix, preferred_element_type=jnp.float32)
    router_slots = jnp.sum(output * cot_rows.astype(jnp.float32), axis=1).astype(jnp.bfloat16)
    scaled = (prob_rows.astype(jnp.float32)[:, None] * cot_rows.astype(jnp.float32)).astype(jnp.bfloat16)
    hidden_grad = jnp.dot(scaled, down_matrix.T, preferred_element_type=jnp.float32)
    up_grad = (hidden_grad * activated).astype(jnp.bfloat16)
    gate_grad = (hidden_grad * up_pre * sigmoid * (1.0 + gate_pre * (1.0 - sigmoid))).astype(jnp.bfloat16)
    routed_grad = (jnp.dot(gate_grad, gate_matrix.T, preferred_element_type=jnp.float32)
                   + jnp.dot(up_grad, up_matrix.T, preferred_element_type=jnp.float32)).astype(jnp.bfloat16)
    scaling = 1.0 / (EXPERTS * CAP)
    grads = jnp.stack([jnp.dot(routed.T, gate_grad, preferred_element_type=jnp.float32),
                       jnp.dot(routed.T, up_grad, preferred_element_type=jnp.float32),
                       jnp.dot(scaled.T, hidden, preferred_element_type=jnp.float32)]) * scaling
    return routed_grad, router_slots, grads


def adasum(stacked):
    for halving in range(LEVELS):
        halfway = stacked.shape[0] // 2
        former = stacked[:halfway]
        latter = stacked[halfway:]
        inner_sum = jnp.sum(former * latter, axis=(2, 3))
        former_sq = jnp.sum(former * former, axis=(2, 3))
        latter_sq = jnp.sum(latter * latter, axis=(2, 3))
        former_coef = 1.0 - inner_sum / (2.0 * (former_sq + epsilon))
        latter_coef = 1.0 - inner_sum / (2.0 * (latter_sq + epsilon))
        stacked = former_coef[:, :, None, None] * former + latter_coef[:, :, None, None] * latter
    return stacked[0]


def take_rows(lookup, indices):
    return jnp.take(lookup, indices, axis=0, mode="fill", fill_value=0)


def reference(tokens, routing, probs, cotangent, w_gate, w_up, w_down):
    blocks = N_DP * N_EXPERT
    choices = TOK_DEV * TOP
    slot_total = EXPERTS * CAP
    destination = jax.vmap(slot_index)(routing.reshape(blocks, TOK_DEV, TOP))

    def invert(dest_row):
        return jnp.full((slot_total,), choices, jnp.int32).at[dest_row].set(jnp.arange(choices, dtype=jnp.int32))

    source = jax.vmap(invert)(destination)
    token_of = jnp.where(source < choices, source // TOP, TOK_DEV).astype(jnp.int32)
    tok_blocks = tokens.reshape(blocks, TOK_DEV, D)
    cot_blocks = cotangent.reshape(blocks, TOK_DEV, D)
    prob_blocks = probs.reshape(blocks, choices)

    def per_expert(expert):
        offset = (expert * CAP).astype(jnp.int32)
        tok_index = lax.dynamic_slice_in_dim(token_of, offset, CAP, 1)
        src_index = lax.dynamic_slice_in_dim(source, offset, CAP, 1)
        routed = jax.vmap(take_rows)(tok_blocks, tok_index).reshape(N_DP, N_EXPERT * CAP, D)
        cot_rows = jax.vmap(take_rows)(cot_blocks, tok_index).reshape(N_DP, N_EXPERT * CAP, D)
        prob_rows = jax.vmap(take_rows)(prob_blocks, src_index).reshape(N_DP, N_EXPERT * CAP)
        gate_matrix = w_gate[expert]
        up_matrix = w_up[expert]
        down_matrix = w_down[expert]

        def one_replica(inputs):
            return expert_pass(inputs[0], inputs[1], inputs[2], gate_matrix, up_matrix, down_matrix)

        routed_grad, router_slots, grads = lax.map(one_replica, (routed, cot_rows, prob_rows))
        return routed_grad, router_slots, adasum(grads)

    routed_grad, router_slots, combined = lax.map(per_expert, jnp.arange(EXPERTS, dtype=jnp.int32))
    block_ids = jnp.arange(blocks, dtype=jnp.int32)
    data_of = (block_ids // N_EXPERT)[:, None]
    peer_of = (block_ids % N_EXPERT)[:, None]
    expert_of = destination // CAP
    slot_of = destination % CAP
    arrived = routed_grad[expert_of, data_of, peer_of * CAP + slot_of]
    input_grad = jnp.sum(arrived.reshape(blocks, TOK_DEV, TOP, D).astype(jnp.float32), axis=2)
    input_grad = input_grad.astype(jnp.bfloat16).reshape(TOKENS, D)
    router_grad = router_slots[expert_of, data_of, peer_of * CAP + slot_of].reshape(TOKENS, TOP)
    grad_gate = combined[:, 0]
    grad_up = combined[:, 1]
    grad_down = jnp.transpose(combined[:, 2], (0, 2, 1))
    return grad_gate, grad_up, grad_down, input_grad, router_grad
```

```python
import functools

import jax
import jax.numpy as jnp
from jax import lax
from jax.experimental import pallas as pl
from jax.experimental.pallas import tpu as pltpu
from jax.sharding import PartitionSpec as P

epsilon = 1e-06
MESH = pl.DeviceIdType.MESH
f32, bf16, i32 = jnp.float32, jnp.bfloat16, jnp.int32
ROWS = 128
LANES = 128


def dot(a, b, ad=1, bd=0):
    return lax.dot_general(a, b, (((ad,), (bd,)), ((), ())), preferred_element_type=f32)


def kernel(
    experts, replicas, cap, capp,
    tok, cot, rout, rout_t, prob_t, wg_hbm, wu_hbm, wd_hbm,
    out_gate, out_up, out_down, out_in, out_router,
    wg, wu, wd, ranks, weights, select, send_tok, send_cot, routed, cotp, scaled,
    gate_pre, up_pre, acts, p_routed, p_scaled, p_acts, ret_send, ret_recv,
    own, part, handed, landed, tot_send, tot_recv,
    w_sem, st_sem, rt_sem, sc_sem, rc_sem, sr_sem, rr_sem,
    yts_sem, ytr_sem, yss_sem, ysr_sem, yas_sem, yar_sem, xs_sem, xr_sem, ts_sem, tr_sem,
):
    me = lax.axis_index("expert")
    dp = lax.axis_index("dp")
    tokens, width = tok.shape
    hidden = wg.shape[1]
    slots = experts * capp
    levels = replicas.bit_length() - 1
    half = width // 2
    bits = [lax.rem(dp // (1 << b), 2) for b in range(levels)]
    mates = [dp + (1 << b) * (1 - 2 * bits[b]) for b in range(levels)]
    top = levels - 1
    order = sorted(range(1, experts), key=lambda i: abs(2 * i - experts))

    def block(index):
        return pl.ds(pl.multiple_of(index * capp, capp), capp)

    loads = [
        pltpu.make_async_copy(src.at[0], dst, w_sem.at[j])
        for j, (src, dst) in enumerate(((wg_hbm, wg), (wu_hbm, wu), (wd_hbm, wd)))
    ]
    for load in loads:
        load.start()

    barrier = pltpu.get_barrier_semaphore()
    for i in range(1, experts):
        pl.semaphore_signal(
            barrier, inc=1, device_id={"expert": lax.rem(me + i, experts)}, device_id_type=MESH
        )
    for mate in mates:
        pl.semaphore_signal(barrier, inc=1, device_id={"dp": mate}, device_id_type=MESH)

    first, second = rout_t[0:1, :], rout_t[1:2, :]
    names = lax.broadcasted_iota(i32, ranks.shape, 0)
    is_first, is_second = names == first, names == second
    member = jnp.where(is_first | is_second, 1.0, 0.0).astype(f32)
    earlier = lax.broadcasted_iota(i32, (tokens, tokens), 0)
    later = lax.broadcasted_iota(i32, (tokens, tokens), 1)
    before = dot(member.astype(bf16), jnp.where(earlier < later, 1.0, 0.0).astype(bf16))
    ranks[...] = jnp.where(member > 0.0, before, -1.0).astype(i32)
    weights[...] = jnp.where(
        is_first, prob_t[0:1, :], jnp.where(is_second, prob_t[1:2, :], 0.0)
    )
    slot = lax.broadcasted_iota(i32, (capp, tokens), 0)

    def picks(expert):
        return slot == ranks[pl.ds(expert, 1), :]

    pl.semaphore_wait(barrier, experts - 1 + levels)

    tok_copies, cot_copies = [], []
    for i in order:
        k = lax.rem(me + i, experts)
        chosen = jnp.where(picks(k), 1.0, 0.0).astype(bf16)
        select[block(k), :] = chosen
        send_tok[block(k), :] = dot(chosen, tok[...]).astype(bf16)
        copy = pltpu.make_async_remote_copy(
            send_tok.at[block(k)], routed.at[block(me)], st_sem.at[i], rt_sem.at[i],
            device_id={"expert": k}, device_id_type=MESH,
        )
        copy.start()
        tok_copies.append(copy)

    def fill_cot(target, k):
        picked = picks(k)
        chosen = jnp.where(picked, 1.0, 0.0).astype(bf16)
        weight = jnp.sum(
            jnp.where(picked, weights[pl.ds(k, 1), :], 0.0), axis=1, keepdims=True
        )
        target[block(k), 0:width] = dot(chosen, cot[...]).astype(bf16)
        target[block(k), width:] = jnp.broadcast_to(weight, (capp, LANES)).astype(bf16)
        return chosen

    for i in order:
        k = lax.rem(me + i, experts)
        fill_cot(send_cot, k)
        copy = pltpu.make_async_remote_copy(
            send_cot.at[block(k)], cotp.at[block(me)], sc_sem.at[i], rc_sem.at[i],
            device_id={"expert": k}, device_id_type=MESH,
        )
        copy.start()
        cot_copies.append(copy)
    mine = fill_cot(cotp, me)
    select[block(me), :] = mine
    routed[block(me), :] = dot(mine, tok[...]).astype(bf16)

    kept_at = pl.multiple_of(bits[top] * half, LANES)
    handed_at = pl.multiple_of((1 - bits[top]) * half, LANES)
    y_copies = []

    def to_mate(source, target, send_sem, recv_sem):
        copy = pltpu.make_async_remote_copy(
            source, target, send_sem, recv_sem, device_id={"dp": mates[top]}, device_id_type=MESH
        )
        copy.start()
        y_copies.append(copy)
        return copy

    tok_to_mate, sca_to_mate, act_to_mate = [], [], {}
    for position, i in enumerate([0] + order):
        k = lax.rem(me + experts - i, experts)
        if i:
            tok_copies[position - 1].wait_recv()
        tok_to_mate.append(to_mate(
            routed.at[block(k), pl.ds(handed_at, half)], p_routed.at[block(k)],
            yts_sem.at[i], ytr_sem.at[i],
        ))

    loads[0].wait()
    loads[1].wait()

    @pl.loop(0, slots // ROWS)
    def _(step):
        rows = pl.ds(pl.multiple_of(step * ROWS, ROWS), ROWS)
        x = routed[rows, :]
        g = dot(x, wg[...])
        u = dot(x, wu[...])
        gate_pre[rows, :] = g
        up_pre[rows, :] = u
        acts[2, rows, :] = (g * jax.nn.sigmoid(g) * u).astype(bf16)

    def send_act(j):
        act_to_mate[j] = to_mate(acts.at[j], p_acts.at[j], yas_sem.at[j], yar_sem.at[j])

    send_act(2)

    for position, i in enumerate([0] + order):
        k = lax.rem(me + experts - i, experts)
        if i:
            cot_copies[position - 1].wait_recv()
        weight = cotp[block(k), width:].astype(f32)[:, 0:1]
        scaled[block(k), :] = (weight * cotp[block(k), 0:width].astype(f32)).astype(bf16)
        sca_to_mate.append(to_mate(
            scaled.at[block(k), pl.ds(handed_at, half)], p_scaled.at[block(k)],
            yss_sem.at[i], ysr_sem.at[i],
        ))

    loads[2].wait()

    @pl.loop(0, slots // ROWS)
    def _(step):
        rows = pl.ds(pl.multiple_of(step * ROWS, ROWS), ROWS)
        hg = dot(scaled[rows, :], wd[...], 1, 1)
        g, u = gate_pre[rows, :], up_pre[rows, :]
        s = jax.nn.sigmoid(g)
        acts[1, rows, :] = (hg * (g * s)).astype(bf16)
        acts[0, rows, :] = (hg * u * s * (1.0 + g * (1.0 - s))).astype(bf16)

    send_act(1)
    send_act(0)

    scaling = 1.0 / (experts * cap)
    tot_rows = lax.broadcasted_iota(i32, (8, LANES), 0)

    def steps_of(level):
        return level + 1

    def step_at(grad, level, step):
        return grad * (levels * (levels + 1) // 2) + level * (level + 1) // 2 + step

    tot_copies, x_copies = [], []

    def share(grad, level, step):
        at = step_at(grad, level, step)
        bit = levels - 1 - level + step
        copy = pltpu.make_async_remote_copy(
            tot_send.at[at], tot_recv.at[at], ts_sem.at[at], tr_sem.at[at],
            device_id={"dp": mates[bit]}, device_id_type=MESH,
        )
        copy.start()
        tot_copies.append(copy)
        return copy

    def begin_totals(grad, level, own_sq, part_sq, inner):
        is_former = bits[levels - 1 - level] == 0
        former = jnp.where(is_former, own_sq, part_sq)
        latter = jnp.where(is_former, part_sq, own_sq)
        packed = jnp.where(
            tot_rows == 0, former, jnp.where(tot_rows == 1, latter, inner)
        )
        tot_send[step_at(grad, level, 0)] = packed
        return share(grad, level, 0)

    def end_totals(grad, level, copy):
        for step in range(steps_of(level)):
            at = step_at(grad, level, step)
            copy.wait_recv()
            total = tot_send[at] + tot_recv[at]
            if step + 1 < steps_of(level):
                tot_send[at + 1] = total
                copy = share(grad, level, step + 1)
        former, latter, inner = total[0:1, 0:1], total[1:2, 0:1], total[2:3, 0:1]
        former_coef = 1.0 - inner / (2.0 * (former + epsilon))
        latter_coef = 1.0 - inner / (2.0 * (latter + epsilon))
        is_former = bits[levels - 1 - level] == 0
        return (
            jnp.where(is_former, former_coef, latter_coef),
            jnp.where(is_former, latter_coef, former_coef),
        )

    def whole(partial):
        return jnp.sum(partial, axis=1, keepdims=True)

    def first_level(grad):
        left, p_left = (scaled, p_scaled) if grad == 2 else (routed, p_routed)
        zero = jnp.zeros((1, hidden), f32)

        def body(step, sums):
            here = pl.multiple_of(step * LANES, LANES)
            there = pl.multiple_of(kept_at + step * LANES, LANES)
            a = dot(left[:, pl.ds(there, LANES)], acts[grad], 0, 0) * scaling
            b = dot(p_left[:, pl.ds(here, LANES)], p_acts[grad], 0, 0) * scaling
            own[grad, pl.ds(here, LANES), :] = a
            part[grad, pl.ds(here, LANES), :] = b
            return (
                sums[0] + jnp.sum(a * a, axis=0, keepdims=True),
                sums[1] + jnp.sum(b * b, axis=0, keepdims=True),
                sums[2] + jnp.sum(a * b, axis=0, keepdims=True),
            )

        sums = lax.fori_loop(0, half // LANES, body, (zero, zero, zero))
        return begin_totals(grad, 0, *[whole(s) for s in sums])

    def x_at(grad, level):
        return grad * max(levels - 1, 1) + level - 1

    def hand_over(grad, level, coefs):
        bit = levels - 1 - level
        size = half >> level
        keep_from = pl.multiple_of(bits[bit] * size, LANES)
        hand_from = pl.multiple_of((1 - bits[bit]) * size, LANES)
        sent = handed.at[grad, pl.ds(half - (half >> (level - 1)), size), :]
        at = x_at(grad, level)

        @pl.loop(0, size // LANES)
        def _(step):
            here = pl.multiple_of(step * LANES, LANES)
            theirs = pl.ds(pl.multiple_of(hand_from + step * LANES, LANES), LANES)
            sent[pl.ds(here, LANES), :] = (
                coefs[0] * own[grad, theirs, :] + coefs[1] * part[grad, theirs, :]
            ).astype(bf16)

        copy = pltpu.make_async_remote_copy(
            sent, landed.at[grad, pl.ds(half - (half >> (level - 1)), size), :],
            xs_sem.at[at], xr_sem.at[at], device_id={"dp": mates[bit]}, device_id_type=MESH,
        )
        copy.start()
        x_copies.append(copy)

        @pl.loop(0, size // LANES)
        def _(step):
            here = pl.multiple_of(step * LANES, LANES)
            ours = pl.ds(pl.multiple_of(keep_from + step * LANES, LANES), LANES)
            own[grad, pl.ds(here, LANES), :] = (
                coefs[0] * own[grad, ours, :] + coefs[1] * part[grad, ours, :]
            )

        return copy

    def next_level(grad, level, copy):
        size = half >> level
        start = half - (half >> (level - 1))
        copy.wait_recv()
        zero = jnp.zeros((1, hidden), f32)

        def body(step, sums):
            here = pl.ds(pl.multiple_of(step * LANES, LANES), LANES)
            a = own[grad, here, :]
            b = landed[grad, pl.ds(pl.multiple_of(start + step * LANES, LANES), LANES), :]
            b = b.astype(f32)
            part[grad, here, :] = b
            return (
                sums[0] + jnp.sum(a * a, axis=0, keepdims=True),
                sums[1] + jnp.sum(b * b, axis=0, keepdims=True),
                sums[2] + jnp.sum(a * b, axis=0, keepdims=True),
            )

        sums = lax.fori_loop(0, size // LANES, body, (zero, zero, zero))
        return begin_totals(grad, level, *[whole(s) for s in sums])

    def finish(grad, coefs):
        size = half >> (levels - 1)
        target = (out_gate, out_up, out_down)[grad]

        @pl.loop(0, size // LANES)
        def _(step):
            here = pl.ds(pl.multiple_of(step * LANES, LANES), LANES)
            value = coefs[0] * own[grad, here, :] + coefs[1] * part[grad, here, :]
            if grad == 2:
                target[0, :, here] = value.T
            else:
                target[0, here, :] = value

    for copy in sca_to_mate + tok_to_mate:
        copy.wait_recv()
    act_to_mate[2].wait_recv()
    pending = {2: first_level(2)}

    @pl.loop(0, slots // ROWS)
    def _(step):
        rows = pl.ds(pl.multiple_of(step * ROWS, ROWS), ROWS)
        back = dot(acts[0, rows, :], wg[...], 1, 1) + dot(acts[1, rows, :], wu[...], 1, 1)
        ret_send[rows, 0:width] = back.astype(bf16)
        output = dot(acts[2, rows, :], wd[...])
        score = jnp.sum(output * cotp[rows, 0:width].astype(f32), axis=1, keepdims=True)
        ret_send[rows, width:] = jnp.broadcast_to(score, (ROWS, LANES)).astype(bf16)

    ret_copies = []
    for i in order:
        k = lax.rem(me + i, experts)
        copy = pltpu.make_async_remote_copy(
            ret_send.at[block(k)], ret_recv.at[block(me)], sr_sem.at[i], rr_sem.at[i],
            device_id={"expert": k}, device_id_type=MESH,
        )
        copy.start()
        ret_copies.append(copy)
    ret_recv[block(me), :] = ret_send[block(me), :]

    moving = {}
    for grad in (2, 1, 0):
        if grad != 2:
            act_to_mate[grad].wait_recv()
            pending[grad] = first_level(grad)
        coefs = end_totals(grad, 0, pending[grad])
        if levels > 1:
            moving[grad] = hand_over(grad, 1, coefs)
        else:
            finish(grad, coefs)
    for level in range(1, levels):
        for grad in (2, 1, 0):
            pending[grad] = next_level(grad, level, moving[grad])
            coefs = end_totals(grad, level, pending[grad])
            if level + 1 < levels:
                moving[grad] = hand_over(grad, level + 1, coefs)
            else:
                finish(grad, coefs)

    for copy in ret_copies:
        copy.wait_recv()

    @pl.loop(0, width // 512)
    def _(step):
        columns = pl.ds(pl.multiple_of(step * 512, 512), 512)
        out_in[:, columns] = dot(select[...], ret_recv[:, columns], 0, 0).astype(bf16)

    chosen_by = rout[...]
    scores = jnp.zeros((tokens, chosen_by.shape[1]), f32)
    for k in range(experts):
        rows = slice(k * capp, (k + 1) * capp)
        score = dot(select[rows, :], ret_recv[rows, width:], 0, 0)
        scores = scores + jnp.where(chosen_by == k, score[:, 0 : chosen_by.shape[1]], 0.0)
    out_router[...] = scores.astype(bf16)

    for copy in tok_copies + cot_copies + ret_copies + y_copies + tot_copies + x_copies:
        copy.wait_send()


def per_device(experts, replicas, tokens, routing, probs, cotangent, w_gate, w_up, w_down):
    rows, top = routing.shape
    width = tokens.shape[1]
    hidden = w_gate.shape[2]
    cap = 5 * rows * top // (4 * experts)
    capp = -(-cap // 16) * 16
    slots = experts * capp
    levels = replicas.bit_length() - 1
    half = width // 2
    shard = width // replicas
    steps = 3 * (levels * (levels + 1) // 2)
    wide = width + LANES
    vm, dma = pltpu.VMEM, pltpu.SemaphoreType.DMA
    in_vmem = pl.BlockSpec(memory_space=pltpu.VMEM)
    in_any = pl.BlockSpec(memory_space=pl.ANY)
    names = max(16, experts)
    return tuple(pl.pallas_call(
        functools.partial(kernel, experts, replicas, cap, capp),
        out_shape=(
            jax.ShapeDtypeStruct((1, shard, hidden), f32),
            jax.ShapeDtypeStruct((1, shard, hidden), f32),
            jax.ShapeDtypeStruct((1, hidden, shard), f32),
            jax.ShapeDtypeStruct((rows, width), bf16),
            jax.ShapeDtypeStruct((rows, top), bf16),
        ),
        in_specs=[in_vmem] * 5 + [in_any] * 3,
        out_specs=(in_vmem,) * 5,
        scratch_shapes=[
            vm((width, hidden), bf16), vm((width, hidden), bf16), vm((hidden, width), bf16),
            vm((names, rows), i32), vm((names, rows), f32), vm((slots, rows), bf16),
            vm((slots, width), bf16), vm((slots, wide), bf16),
            vm((slots, width), bf16), vm((slots, wide), bf16), vm((slots, width), bf16),
            vm((slots, hidden), f32), vm((slots, hidden), f32), vm((3, slots, hidden), bf16),
            vm((slots, half), bf16), vm((slots, half), bf16), vm((3, slots, hidden), bf16),
            vm((slots, wide), bf16), vm((slots, wide), bf16),
            vm((3, half, hidden), f32), vm((3, half, hidden), f32),
            vm((3, half, hidden), bf16), vm((3, half, hidden), bf16),
            vm((steps, 8, LANES), f32), vm((steps, 8, LANES), f32),
            dma((3,)),
        ] + [dma((experts,))] * 10 + [dma((3,))] * 2
        + [dma((3 * max(levels - 1, 1),))] * 2 + [dma((steps,))] * 2,
        compiler_params=pltpu.CompilerParams(
            collective_id=0, has_side_effects=True, vmem_limit_bytes=67_000_000
        ),
        name="adasum_moe",
    )(
        tokens, cotangent, routing, routing.T, probs.T.astype(f32), w_gate, w_up, w_down
    ))


def solution(mesh):
    rows = P(("dp", "expert"), None)
    return jax.shard_map(
        functools.partial(per_device, mesh.shape["expert"], mesh.shape["dp"]),
        mesh=mesh,
        in_specs=(rows,) * 4 + (P("expert", None, None),) * 3,
        out_specs=(
            P("expert", "dp", None),
            P("expert", "dp", None),
            P("expert", None, "dp"),
            rows,
            rows,
        ),
        check_vma=False,
    )
```

```python
import functools

import jax
import jax.numpy as jnp
from jax import lax
from jax.experimental import pallas as pl
from jax.experimental.pallas import tpu as pltpu
from jax.sharding import PartitionSpec as P

epsilon = 1e-06
MESH = pl.DeviceIdType.MESH
f32, bf16, i32 = jnp.float32, jnp.bfloat16, jnp.int32
ROWS = 128
LANES = 128


def dot(a, b, ad=1, bd=0):
    return lax.dot_general(a, b, (((ad,), (bd,)), ((), ())), preferred_element_type=f32)


def halving_kernel(
    experts, replicas, cap, capp,
    tok, cot, rout, rout_t, prob_t, wg_hbm, wu_hbm, wd_hbm,
    out_gate, out_up, out_down, out_in, out_router,
    wg, wu, wd, ranks, weights, select, send_tok, send_cot, routed, cotp, scaled,
    gate_pre, up_pre, acts, p_routed, p_scaled, p_acts, ret_send, ret_recv,
    own, part, handed, landed, tot_send, tot_recv,
    w_sem, st_sem, rt_sem, sc_sem, rc_sem, sr_sem, rr_sem,
    yts_sem, ytr_sem, yss_sem, ysr_sem, yas_sem, yar_sem, xs_sem, xr_sem, ts_sem, tr_sem,
):
    me = lax.axis_index("expert")
    dp = lax.axis_index("dp")
    tokens, width = tok.shape
    hidden = wg.shape[1]
    slots = experts * capp
    levels = replicas.bit_length() - 1
    half = width // 2
    bits = [lax.rem(dp // (1 << b), 2) for b in range(levels)]
    mates = [dp + (1 << b) * (1 - 2 * bits[b]) for b in range(levels)]
    top = levels - 1
    order = sorted(range(1, experts), key=lambda i: abs(2 * i - experts))

    def block(index):
        return pl.ds(pl.multiple_of(index * capp, capp), capp)

    loads = [
        pltpu.make_async_copy(src.at[0], dst, w_sem.at[j])
        for j, (src, dst) in enumerate(((wg_hbm, wg), (wu_hbm, wu), (wd_hbm, wd)))
    ]
    for load in loads:
        load.start()

    barrier = pltpu.get_barrier_semaphore()
    for i in range(1, experts):
        pl.semaphore_signal(
            barrier, inc=1, device_id={"expert": lax.rem(me + i, experts)}, device_id_type=MESH
        )
    for mate in mates:
        pl.semaphore_signal(barrier, inc=1, device_id={"dp": mate}, device_id_type=MESH)

    first, second = rout_t[0:1, :], rout_t[1:2, :]
    names = lax.broadcasted_iota(i32, ranks.shape, 0)
    is_first, is_second = names == first, names == second
    member = jnp.where(is_first | is_second, 1.0, 0.0).astype(f32)
    earlier = lax.broadcasted_iota(i32, (tokens, tokens), 0)
    later = lax.broadcasted_iota(i32, (tokens, tokens), 1)
    before = dot(member.astype(bf16), jnp.where(earlier < later, 1.0, 0.0).astype(bf16))
    ranks[...] = jnp.where(member > 0.0, before, -1.0).astype(i32)
    weights[...] = jnp.where(
        is_first, prob_t[0:1, :], jnp.where(is_second, prob_t[1:2, :], 0.0)
    )
    slot = lax.broadcasted_iota(i32, (capp, tokens), 0)

    def picks(expert):
        return slot == ranks[pl.ds(expert, 1), :]

    pl.semaphore_wait(barrier, experts - 1 + levels)

    tok_copies, cot_copies = [], []
    for i in order:
        k = lax.rem(me + i, experts)
        chosen = jnp.where(picks(k), 1.0, 0.0).astype(bf16)
        select[block(k), :] = chosen
        send_tok[block(k), :] = dot(chosen, tok[...]).astype(bf16)
        copy = pltpu.make_async_remote_copy(
            send_tok.at[block(k)], routed.at[block(me)], st_sem.at[i], rt_sem.at[i],
            device_id={"expert": k}, device_id_type=MESH,
        )
        copy.start()
        tok_copies.append(copy)

    def fill_cot(target, k):
        picked = picks(k)
        chosen = jnp.where(picked, 1.0, 0.0).astype(bf16)
        weight = jnp.sum(
            jnp.where(picked, weights[pl.ds(k, 1), :], 0.0), axis=1, keepdims=True
        )
        target[block(k), 0:width] = dot(chosen, cot[...]).astype(bf16)
        target[block(k), width:] = jnp.broadcast_to(weight, (capp, LANES)).astype(bf16)
        return chosen

    for i in order:
        k = lax.rem(me + i, experts)
        fill_cot(send_cot, k)
        copy = pltpu.make_async_remote_copy(
            send_cot.at[block(k)], cotp.at[block(me)], sc_sem.at[i], rc_sem.at[i],
            device_id={"expert": k}, device_id_type=MESH,
        )
        copy.start()
        cot_copies.append(copy)
    mine = fill_cot(cotp, me)
    select[block(me), :] = mine
    routed[block(me), :] = dot(mine, tok[...]).astype(bf16)

    kept_at = pl.multiple_of(bits[top] * half, LANES)
    handed_at = pl.multiple_of((1 - bits[top]) * half, LANES)
    y_copies = []

    def to_mate(source, target, send_sem, recv_sem):
        copy = pltpu.make_async_remote_copy(
            source, target, send_sem, recv_sem, device_id={"dp": mates[top]}, device_id_type=MESH
        )
        copy.start()
        y_copies.append(copy)
        return copy

    tok_to_mate, sca_to_mate, act_to_mate = [], [], {}
    for position, i in enumerate([0] + order):
        k = lax.rem(me + experts - i, experts)
        if i:
            tok_copies[position - 1].wait_recv()
        tok_to_mate.append(to_mate(
            routed.at[block(k), pl.ds(handed_at, half)], p_routed.at[block(k)],
            yts_sem.at[i], ytr_sem.at[i],
        ))

    loads[0].wait()
    loads[1].wait()

    @pl.loop(0, slots // ROWS)
    def _(step):
        rows = pl.ds(pl.multiple_of(step * ROWS, ROWS), ROWS)
        x = routed[rows, :]
        g = dot(x, wg[...])
        u = dot(x, wu[...])
        gate_pre[rows, :] = g
        up_pre[rows, :] = u
        acts[2, rows, :] = (g * jax.nn.sigmoid(g) * u).astype(bf16)

    def send_act(j):
        act_to_mate[j] = to_mate(acts.at[j], p_acts.at[j], yas_sem.at[j], yar_sem.at[j])

    send_act(2)

    for position, i in enumerate([0] + order):
        k = lax.rem(me + experts - i, experts)
        if i:
            cot_copies[position - 1].wait_recv()
        weight = cotp[block(k), width:].astype(f32)[:, 0:1]
        scaled[block(k), :] = (weight * cotp[block(k), 0:width].astype(f32)).astype(bf16)
        sca_to_mate.append(to_mate(
            scaled.at[block(k), pl.ds(handed_at, half)], p_scaled.at[block(k)],
            yss_sem.at[i], ysr_sem.at[i],
        ))

    loads[2].wait()

    @pl.loop(0, slots // ROWS)
    def _(step):
        rows = pl.ds(pl.multiple_of(step * ROWS, ROWS), ROWS)
        hg = dot(scaled[rows, :], wd[...], 1, 1)
        g, u = gate_pre[rows, :], up_pre[rows, :]
        s = jax.nn.sigmoid(g)
        acts[1, rows, :] = (hg * (g * s)).astype(bf16)
        acts[0, rows, :] = (hg * u * s * (1.0 + g * (1.0 - s))).astype(bf16)

    send_act(1)
    send_act(0)

    scaling = 1.0 / (experts * cap)
    tot_rows = lax.broadcasted_iota(i32, (8, LANES), 0)

    def steps_of(level):
        return level + 1

    def step_at(grad, level, step):
        return grad * (levels * (levels + 1) // 2) + level * (level + 1) // 2 + step

    tot_copies, x_copies = [], []

    def share(grad, level, step):
        at = step_at(grad, level, step)
        bit = levels - 1 - level + step
        copy = pltpu.make_async_remote_copy(
            tot_send.at[at], tot_recv.at[at], ts_sem.at[at], tr_sem.at[at],
            device_id={"dp": mates[bit]}, device_id_type=MESH,
        )
        copy.start()
        tot_copies.append(copy)
        return copy

    def begin_totals(grad, level, own_sq, part_sq, inner):
        is_former = bits[levels - 1 - level] == 0
        former = jnp.where(is_former, own_sq, part_sq)
        latter = jnp.where(is_former, part_sq, own_sq)
        packed = jnp.where(
            tot_rows == 0, former, jnp.where(tot_rows == 1, latter, inner)
        )
        tot_send[step_at(grad, level, 0)] = packed
        return share(grad, level, 0)

    def end_totals(grad, level, copy):
        for step in range(steps_of(level)):
            at = step_at(grad, level, step)
            copy.wait_recv()
            total = tot_send[at] + tot_recv[at]
            if step + 1 < steps_of(level):
                tot_send[at + 1] = total
                copy = share(grad, level, step + 1)
        former, latter, inner = total[0:1, 0:1], total[1:2, 0:1], total[2:3, 0:1]
        former_coef = 1.0 - inner / (2.0 * (former + epsilon))
        latter_coef = 1.0 - inner / (2.0 * (latter + epsilon))
        is_former = bits[levels - 1 - level] == 0
        return (
            jnp.where(is_former, former_coef, latter_coef),
            jnp.where(is_former, latter_coef, former_coef),
        )

    def whole(partial):
        return jnp.sum(partial, axis=1, keepdims=True)

    def first_level(grad):
        left, p_left = (scaled, p_scaled) if grad == 2 else (routed, p_routed)
        zero = jnp.zeros((1, hidden), f32)

        def body(step, sums):
            here = pl.multiple_of(step * LANES, LANES)
            there = pl.multiple_of(kept_at + step * LANES, LANES)
            a = dot(left[:, pl.ds(there, LANES)], acts[grad], 0, 0) * scaling
            b = dot(p_left[:, pl.ds(here, LANES)], p_acts[grad], 0, 0) * scaling
            own[grad, pl.ds(here, LANES), :] = a
            part[grad, pl.ds(here, LANES), :] = b
            return (
                sums[0] + jnp.sum(a * a, axis=0, keepdims=True),
                sums[1] + jnp.sum(b * b, axis=0, keepdims=True),
                sums[2] + jnp.sum(a * b, axis=0, keepdims=True),
            )

        sums = lax.fori_loop(0, half // LANES, body, (zero, zero, zero))
        return begin_totals(grad, 0, *[whole(s) for s in sums])

    def x_at(grad, level):
        return grad * max(levels - 1, 1) + level - 1

    def hand_over(grad, level, coefs):
        bit = levels - 1 - level
        size = half >> level
        keep_from = pl.multiple_of(bits[bit] * size, LANES)
        hand_from = pl.multiple_of((1 - bits[bit]) * size, LANES)
        sent = handed.at[grad, pl.ds(half - (half >> (level - 1)), size), :]
        at = x_at(grad, level)

        @pl.loop(0, size // LANES)
        def _(step):
            here = pl.multiple_of(step * LANES, LANES)
            theirs = pl.ds(pl.multiple_of(hand_from + step * LANES, LANES), LANES)
            sent[pl.ds(here, LANES), :] = (
                coefs[0] * own[grad, theirs, :] + coefs[1] * part[grad, theirs, :]
            ).astype(bf16)

        copy = pltpu.make_async_remote_copy(
            sent, landed.at[grad, pl.ds(half - (half >> (level - 1)), size), :],
            xs_sem.at[at], xr_sem.at[at], device_id={"dp": mates[bit]}, device_id_type=MESH,
        )
        copy.start()
        x_copies.append(copy)

        @pl.loop(0, size // LANES)
        def _(step):
            here = pl.multiple_of(step * LANES, LANES)
            ours = pl.ds(pl.multiple_of(keep_from + step * LANES, LANES), LANES)
            own[grad, pl.ds(here, LANES), :] = (
                coefs[0] * own[grad, ours, :] + coefs[1] * part[grad, ours, :]
            )

        return copy

    def next_level(grad, level, copy):
        size = half >> level
        start = half - (half >> (level - 1))
        copy.wait_recv()
        zero = jnp.zeros((1, hidden), f32)

        def body(step, sums):
            here = pl.ds(pl.multiple_of(step * LANES, LANES), LANES)
            a = own[grad, here, :]
            b = landed[grad, pl.ds(pl.multiple_of(start + step * LANES, LANES), LANES), :]
            b = b.astype(f32)
            part[grad, here, :] = b
            return (
                sums[0] + jnp.sum(a * a, axis=0, keepdims=True),
                sums[1] + jnp.sum(b * b, axis=0, keepdims=True),
                sums[2] + jnp.sum(a * b, axis=0, keepdims=True),
            )

        sums = lax.fori_loop(0, size // LANES, body, (zero, zero, zero))
        return begin_totals(grad, level, *[whole(s) for s in sums])

    def finish(grad, coefs):
        size = half >> (levels - 1)
        target = (out_gate, out_up, out_down)[grad]

        @pl.loop(0, size // LANES)
        def _(step):
            here = pl.ds(pl.multiple_of(step * LANES, LANES), LANES)
            value = coefs[0] * own[grad, here, :] + coefs[1] * part[grad, here, :]
            if grad == 2:
                target[0, :, here] = value.T
            else:
                target[0, here, :] = value

    for copy in sca_to_mate + tok_to_mate:
        copy.wait_recv()
    act_to_mate[2].wait_recv()
    pending = {2: first_level(2)}

    @pl.loop(0, slots // ROWS)
    def _(step):
        rows = pl.ds(pl.multiple_of(step * ROWS, ROWS), ROWS)
        back = dot(acts[0, rows, :], wg[...], 1, 1) + dot(acts[1, rows, :], wu[...], 1, 1)
        ret_send[rows, 0:width] = back.astype(bf16)
        output = dot(acts[2, rows, :], wd[...])
        score = jnp.sum(output * cotp[rows, 0:width].astype(f32), axis=1, keepdims=True)
        ret_send[rows, width:] = jnp.broadcast_to(score, (ROWS, LANES)).astype(bf16)

    ret_copies = []
    for i in order:
        k = lax.rem(me + i, experts)
        copy = pltpu.make_async_remote_copy(
            ret_send.at[block(k)], ret_recv.at[block(me)], sr_sem.at[i], rr_sem.at[i],
            device_id={"expert": k}, device_id_type=MESH,
        )
        copy.start()
        ret_copies.append(copy)
    ret_recv[block(me), :] = ret_send[block(me), :]

    moving = {}
    for grad in (2, 1, 0):
        if grad != 2:
            act_to_mate[grad].wait_recv()
            pending[grad] = first_level(grad)
        coefs = end_totals(grad, 0, pending[grad])
        if levels > 1:
            moving[grad] = hand_over(grad, 1, coefs)
        else:
            finish(grad, coefs)
    for level in range(1, levels):
        for grad in (2, 1, 0):
            pending[grad] = next_level(grad, level, moving[grad])
            coefs = end_totals(grad, level, pending[grad])
            if level + 1 < levels:
                moving[grad] = hand_over(grad, level + 1, coefs)
            else:
                finish(grad, coefs)

    for copy in ret_copies:
        copy.wait_recv()

    @pl.loop(0, width // 512)
    def _(step):
        columns = pl.ds(pl.multiple_of(step * 512, 512), 512)
        out_in[:, columns] = dot(select[...], ret_recv[:, columns], 0, 0).astype(bf16)

    chosen_by = rout[...]
    scores = jnp.zeros((tokens, chosen_by.shape[1]), f32)
    for k in range(experts):
        rows = slice(k * capp, (k + 1) * capp)
        score = dot(select[rows, :], ret_recv[rows, width:], 0, 0)
        scores = scores + jnp.where(chosen_by == k, score[:, 0 : chosen_by.shape[1]], 0.0)
    out_router[...] = scores.astype(bf16)

    for copy in tok_copies + cot_copies + ret_copies + y_copies + tot_copies + x_copies:
        copy.wait_send()


def kernel(
    experts, replicas, cap, capp,
    tok, cot, rout, rout_t, prob_t, wg_hbm, wu_hbm, wd_hbm,
    out_gate, out_up, out_down, out_in, out_router,
    wg, wu, wd, ranks, weights, select, send_tok, send_cot, routed, cotp, scaled,
    gate_pre, up_pre, acts, p_routed, p_scaled, p_acts, ret_send, ret_recv,
    grads, gram_send, gram_recv,
    w_sem, st_sem, rt_sem, sc_sem, rc_sem, sr_sem, rr_sem,
    yts_sem, ytr_sem, yss_sem, ysr_sem, yas_sem, yar_sem, gs_sem, gr_sem,
):
    me = lax.axis_index("expert")
    dp = lax.axis_index("dp")
    tokens, width = tok.shape
    hidden = wg.shape[1]
    slots = experts * capp
    levels = replicas.bit_length() - 1
    quarter = width // replicas
    bits = [lax.rem(dp // (1 << b), 2) for b in range(levels)]
    mates = [
        dp + sum((1 << b) * (1 - 2 * bits[b]) for b in range(levels) if j >> b & 1)
        for j in range(replicas)
    ]
    others = range(1, replicas)
    order = sorted(range(1, experts), key=lambda i: abs(2 * i - experts))

    def block(index):
        return pl.ds(pl.multiple_of(index * capp, capp), capp)

    loads = [
        pltpu.make_async_copy(src.at[0], dst, w_sem.at[j])
        for j, (src, dst) in enumerate(((wg_hbm, wg), (wu_hbm, wu), (wd_hbm, wd)))
    ]
    for load in loads:
        load.start()

    barrier = pltpu.get_barrier_semaphore()
    for i in range(1, experts):
        pl.semaphore_signal(
            barrier, inc=1, device_id={"expert": lax.rem(me + i, experts)}, device_id_type=MESH
        )
    for mate in mates[1:]:
        pl.semaphore_signal(barrier, inc=1, device_id={"dp": mate}, device_id_type=MESH)

    first, second = rout_t[0:1, :], rout_t[1:2, :]
    names = lax.broadcasted_iota(i32, ranks.shape, 0)
    is_first, is_second = names == first, names == second
    member = jnp.where(is_first | is_second, 1.0, 0.0).astype(f32)
    earlier = lax.broadcasted_iota(i32, (tokens, tokens), 0)
    later = lax.broadcasted_iota(i32, (tokens, tokens), 1)
    before = dot(member.astype(bf16), jnp.where(earlier < later, 1.0, 0.0).astype(bf16))
    ranks[...] = jnp.where(member > 0.0, before, -1.0).astype(i32)
    weights[...] = jnp.where(
        is_first, prob_t[0:1, :], jnp.where(is_second, prob_t[1:2, :], 0.0)
    )
    slot = lax.broadcasted_iota(i32, (capp, tokens), 0)

    def picks(expert):
        return slot == ranks[pl.ds(expert, 1), :]

    pl.semaphore_wait(barrier, experts + replicas - 2)

    tok_copies, cot_copies = [], []
    for i in order:
        k = lax.rem(me + i, experts)
        chosen = jnp.where(picks(k), 1.0, 0.0).astype(bf16)
        select[block(k), :] = chosen
        send_tok[block(k), :] = dot(chosen, tok[...]).astype(bf16)
        copy = pltpu.make_async_remote_copy(
            send_tok.at[block(k)], routed.at[block(me)], st_sem.at[i], rt_sem.at[i],
            device_id={"expert": k}, device_id_type=MESH,
        )
        copy.start()
        tok_copies.append(copy)

    def fill_cot(target, k):
        picked = picks(k)
        chosen = jnp.where(picked, 1.0, 0.0).astype(bf16)
        weight = jnp.sum(
            jnp.where(picked, weights[pl.ds(k, 1), :], 0.0), axis=1, keepdims=True
        )
        target[block(k), 0:width] = dot(chosen, cot[...]).astype(bf16)
        target[block(k), width:] = jnp.broadcast_to(weight, (capp, LANES)).astype(bf16)
        return chosen

    for i in order:
        k = lax.rem(me + i, experts)
        fill_cot(send_cot, k)
        copy = pltpu.make_async_remote_copy(
            send_cot.at[block(k)], cotp.at[block(me)], sc_sem.at[i], rc_sem.at[i],
            device_id={"expert": k}, device_id_type=MESH,
        )
        copy.start()
        cot_copies.append(copy)
    mine = fill_cot(cotp, me)
    select[block(me), :] = mine
    routed[block(me), :] = dot(mine, tok[...]).astype(bf16)

    y_copies = []

    def columns_of(mate):
        return pl.ds(pl.multiple_of(mate * quarter, LANES), quarter)

    def to_mate(j, source, target, send_sem, recv_sem):
        copy = pltpu.make_async_remote_copy(
            source, target, send_sem, recv_sem, device_id={"dp": mates[j]}, device_id_type=MESH
        )
        copy.start()
        y_copies.append(copy)
        return copy

    tok_to_mate, sca_to_mate, act_to_mate = [], [], {}
    for position, i in enumerate([0] + order):
        k = lax.rem(me + experts - i, experts)
        if i:
            tok_copies[position - 1].wait_recv()
        for j in others:
            tok_to_mate.append(to_mate(
                j, routed.at[block(k), columns_of(mates[j])], p_routed.at[j, block(k)],
                yts_sem.at[j, i], ytr_sem.at[j, i],
            ))

    loads[0].wait()
    loads[1].wait()

    @pl.loop(0, slots // ROWS)
    def _(step):
        rows = pl.ds(pl.multiple_of(step * ROWS, ROWS), ROWS)
        x = routed[rows, :]
        g = dot(x, wg[...])
        u = dot(x, wu[...])
        gate_pre[rows, :] = g
        up_pre[rows, :] = u
        acts[2, rows, :] = (g * jax.nn.sigmoid(g) * u).astype(bf16)

    def send_act(grad, j, source=None):
        act_to_mate[grad, source or j] = to_mate(
            j, p_acts.at[grad, source ^ j] if source else acts.at[grad],
            p_acts.at[grad, source or j],
            yas_sem.at[grad, source or j], yar_sem.at[grad, source or j],
        )

    for j in others:
        send_act(2, j)

    for position, i in enumerate([0] + order):
        k = lax.rem(me + experts - i, experts)
        if i:
            cot_copies[position - 1].wait_recv()
        weight = cotp[block(k), width:].astype(f32)[:, 0:1]
        scaled[block(k), :] = (weight * cotp[block(k), 0:width].astype(f32)).astype(bf16)
        for j in others:
            sca_to_mate.append(to_mate(
                j, scaled.at[block(k), columns_of(mates[j])], p_scaled.at[j, block(k)],
                yss_sem.at[j, i], ysr_sem.at[j, i],
            ))

    loads[2].wait()

    @pl.loop(0, slots // ROWS)
    def _(step):
        rows = pl.ds(pl.multiple_of(step * ROWS, ROWS), ROWS)
        hg = dot(scaled[rows, :], wd[...], 1, 1)
        g, u = gate_pre[rows, :], up_pre[rows, :]
        s = jax.nn.sigmoid(g)
        acts[1, rows, :] = (hg * (g * s)).astype(bf16)
        acts[0, rows, :] = (hg * u * s * (1.0 + g * (1.0 - s))).astype(bf16)

    relayed = replicas == 4
    near = (1, 2) if relayed else others
    for grad in (1, 0):
        for j in near:
            send_act(grad, j)

    scaling = 1.0 / (experts * cap)
    pairs = [(i, j) for i in range(replicas) for j in range(i, replicas)]

    def grad_of(grad, j):
        left, p_left = (scaled, p_scaled) if grad == 2 else (routed, p_routed)

        @pl.loop(0, quarter // LANES)
        def _(step):
            here = pl.ds(pl.multiple_of(step * LANES, LANES), LANES)
            if j:
                x, y = p_left[j, :, here], p_acts[grad, j]
            else:
                there = pl.multiple_of(dp * quarter + step * LANES, LANES)
                x, y = left[:, pl.ds(there, LANES)], acts[grad]
            grads[grad, j, here, :] = dot(x, y, 0, 0) * scaling

    def gram_of(grad):
        def body(step, sums):
            here = pl.ds(pl.multiple_of(step * 8, 8), 8)
            held = [grads[grad, j, here, :] for j in range(replicas)]
            return tuple(s + held[i] * held[j] for s, (i, j) in zip(sums, pairs))

        zero = jnp.zeros((8, hidden), f32)
        sums = lax.fori_loop(0, quarter // 8, body, (zero,) * len(pairs))
        for row, total in enumerate(sums):
            total = jnp.sum(jnp.sum(total, axis=0, keepdims=True), axis=1, keepdims=True)
            gram_send[grad, row : row + 1, :] = jnp.broadcast_to(total, (1, LANES))

    def combine(grad):
        def entry(i, j):
            total = 0.0
            for m in range(replicas):
                row = pairs.index(tuple(sorted((i ^ m, j ^ m))))
                held = gram_recv[m, grad, row : row + 1, :] if m else gram_send[grad, row : row + 1, :]
                total = total + held
            return total

        gram = {pair: entry(*pair) for pair in pairs}

        def product(left, right):
            return sum(
                left[i] * right[j] * gram[min(i, j), max(i, j)] for i in left for j in right
            )

        vectors = [{j: jnp.ones((1, LANES), f32)} for j in range(replicas)]
        while len(vectors) > 1:
            count = len(vectors) // 2
            joined = []
            for j in range(count):
                a, b = vectors[j], vectors[j + count]
                inner = product(a, b)
                na = jnp.maximum(product(a, a), 0.0)
                nb = jnp.maximum(product(b, b), 0.0)
                ca = 1.0 - inner / (2.0 * (na + epsilon))
                cb = 1.0 - inner / (2.0 * (nb + epsilon))
                joined.append({
                    **{i: ca * c for i, c in a.items()}, **{i: cb * c for i, c in b.items()}
                })
            vectors = joined
        coefs = [vectors[0][j][:, 0:1] for j in range(replicas)]
        target = (out_gate, out_up, out_down)[grad]

        @pl.loop(0, quarter // LANES)
        def _(step):
            here = pl.ds(pl.multiple_of(step * LANES, LANES), LANES)
            value = coefs[0] * grads[grad, 0, here, :]
            for j in others:
                value = value + coefs[j] * grads[grad, j, here, :]
            if grad == 2:
                target[0, :, here] = value.T
            else:
                target[0, here, :] = value

    @pl.loop(0, slots // ROWS)
    def _(step):
        rows = pl.ds(pl.multiple_of(step * ROWS, ROWS), ROWS)
        back = dot(acts[0, rows, :], wg[...], 1, 1) + dot(acts[1, rows, :], wu[...], 1, 1)
        ret_send[rows, 0:width] = back.astype(bf16)
        output = dot(acts[2, rows, :], wd[...])
        score = jnp.sum(output * cotp[rows, 0:width].astype(f32), axis=1, keepdims=True)
        ret_send[rows, width:] = jnp.broadcast_to(score, (ROWS, LANES)).astype(bf16)

    ret_copies = []
    for i in order:
        k = lax.rem(me + i, experts)
        copy = pltpu.make_async_remote_copy(
            ret_send.at[block(k)], ret_recv.at[block(me)], sr_sem.at[i], rr_sem.at[i],
            device_id={"expert": k}, device_id_type=MESH,
        )
        copy.start()
        ret_copies.append(copy)
    ret_recv[block(me), :] = ret_send[block(me), :]

    for copy in sca_to_mate + tok_to_mate:
        copy.wait_recv()
    for grad in (2, 1, 0):
        grad_of(grad, 0)
    for j in others:
        act_to_mate[2, j].wait_recv()
        grad_of(2, j)
    gram_of(2)
    for grad, far in ((1, 1), (0, 2)):
        for j in near:
            act_to_mate[grad, j].wait_recv()
        if relayed:
            send_act(grad, far, 3)
        for j in near:
            grad_of(grad, j)
    for grad in (1, 0):
        if relayed:
            act_to_mate[grad, 3].wait_recv()
            grad_of(grad, 3)
        gram_of(grad)
    gram_copies = []
    for j in others:
        copy = pltpu.make_async_remote_copy(
            gram_send, gram_recv.at[j], gs_sem.at[j], gr_sem.at[j],
            device_id={"dp": mates[j]}, device_id_type=MESH,
        )
        copy.start()
        gram_copies.append(copy)
    for copy in gram_copies:
        copy.wait_recv()
    for grad in (2, 1, 0):
        combine(grad)

    for copy in ret_copies:
        copy.wait_recv()

    @pl.loop(0, width // 512)
    def _(step):
        columns = pl.ds(pl.multiple_of(step * 512, 512), 512)
        out_in[:, columns] = dot(select[...], ret_recv[:, columns], 0, 0).astype(bf16)

    chosen_by = rout[...]
    scores = jnp.zeros((tokens, chosen_by.shape[1]), f32)
    for k in range(experts):
        rows = slice(k * capp, (k + 1) * capp)
        score = dot(select[rows, :], ret_recv[rows, width:], 0, 0)
        scores = scores + jnp.where(chosen_by == k, score[:, 0 : chosen_by.shape[1]], 0.0)
    out_router[...] = scores.astype(bf16)

    for copy in tok_copies + cot_copies + ret_copies + y_copies + gram_copies:
        copy.wait_send()


def per_device(experts, replicas, tokens, routing, probs, cotangent, w_gate, w_up, w_down):
    rows, top = routing.shape
    width = tokens.shape[1]
    hidden = w_gate.shape[2]
    cap = 5 * rows * top // (4 * experts)
    capp = -(-cap // 16) * 16
    slots = experts * capp
    levels = replicas.bit_length() - 1
    half = width // 2
    shard = width // replicas
    direct = replicas <= 4
    steps = 3 * (levels * (levels + 1) // 2)
    wide = width + LANES
    vm, dma = pltpu.VMEM, pltpu.SemaphoreType.DMA
    in_vmem = pl.BlockSpec(memory_space=pltpu.VMEM)
    in_any = pl.BlockSpec(memory_space=pl.ANY)
    names = max(16, experts)
    grams = -(-replicas * (replicas + 1) // 16) * 8
    return tuple(pl.pallas_call(
        functools.partial(kernel if direct else halving_kernel, experts, replicas, cap, capp),
        out_shape=(
            jax.ShapeDtypeStruct((1, shard, hidden), f32),
            jax.ShapeDtypeStruct((1, shard, hidden), f32),
            jax.ShapeDtypeStruct((1, hidden, shard), f32),
            jax.ShapeDtypeStruct((rows, width), bf16),
            jax.ShapeDtypeStruct((rows, top), bf16),
        ),
        in_specs=[in_vmem] * 5 + [in_any] * 3,
        out_specs=(in_vmem,) * 5,
        scratch_shapes=[
            vm((width, hidden), bf16), vm((width, hidden), bf16), vm((hidden, width), bf16),
            vm((names, rows), i32), vm((names, rows), f32), vm((slots, rows), bf16),
            vm((slots, width), bf16), vm((slots, wide), bf16),
            vm((slots, width), bf16), vm((slots, wide), bf16), vm((slots, width), bf16),
            vm((slots, hidden), f32), vm((slots, hidden), f32), vm((3, slots, hidden), bf16),
        ] + ([
            vm((replicas, slots, shard), bf16), vm((replicas, slots, shard), bf16),
            vm((3, replicas, slots, hidden), bf16),
        ] if direct else [
            vm((slots, half), bf16), vm((slots, half), bf16), vm((3, slots, hidden), bf16),
        ]) + [
            vm((slots, wide), bf16), vm((slots, wide), bf16),
        ] + ([
            vm((3, replicas, shard, hidden), f32),
            vm((3, grams, LANES), f32), vm((replicas, 3, grams, LANES), f32),
        ] if direct else [
            vm((3, half, hidden), f32), vm((3, half, hidden), f32),
            vm((3, half, hidden), bf16), vm((3, half, hidden), bf16),
            vm((steps, 8, LANES), f32), vm((steps, 8, LANES), f32),
        ]) + [dma((3,))] + [dma((experts,))] * 6 + ([
            dma((replicas, experts)), dma((replicas, experts)),
            dma((replicas, experts)), dma((replicas, experts)),
            dma((3, replicas)), dma((3, replicas)), dma((replicas,)), dma((replicas,)),
        ] if direct else [dma((experts,))] * 4 + [dma((3,))] * 2
            + [dma((3 * max(levels - 1, 1),))] * 2 + [dma((steps,))] * 2),
        compiler_params=pltpu.CompilerParams(
            collective_id=0, has_side_effects=True, vmem_limit_bytes=67_000_000
        ),
        name="adasum_moe",
    )(
        tokens, cotangent, routing, routing.T, probs.T.astype(f32), w_gate, w_up, w_down
    ))


def solution(mesh):
    rows = P(("dp", "expert"), None)
    return jax.shard_map(
        functools.partial(per_device, mesh.shape["expert"], mesh.shape["dp"]),
        mesh=mesh,
        in_specs=(rows,) * 4 + (P("expert", None, None),) * 3,
        out_specs=(
            P("expert", "dp", None),
            P("expert", "dp", None),
            P("expert", None, "dp"),
            rows,
            rows,
        ),
        check_vma=False,
    )
```

```python
import functools

import jax
import jax.numpy as jnp
from jax import lax
from jax.experimental import pallas as pl
from jax.experimental.pallas import tpu as pltpu
from jax.sharding import PartitionSpec as P

epsilon = 1e-06
MESH = pl.DeviceIdType.MESH
f32, bf16, i32 = jnp.float32, jnp.bfloat16, jnp.int32
ROWS = 128
LANES = 128


def dot(a, b, ad=1, bd=0):
    return lax.dot_general(a, b, (((ad,), (bd,)), ((), ())), preferred_element_type=f32)


def halving_kernel(
    experts, replicas, cap, capp,
    tok, cot, rout, rout_t, prob_t, wg_hbm, wu_hbm, wd_hbm,
    out_gate, out_up, out_down, out_in, out_router,
    wg, wu, wd, ranks, weights, select, send_tok, send_cot, routed, cotp, scaled,
    gate_pre, up_pre, acts, p_routed, p_scaled, p_acts, ret_send, ret_recv,
    own, part, handed, landed, tot_send, tot_recv,
    w_sem, st_sem, rt_sem, sc_sem, rc_sem, sr_sem, rr_sem,
    yts_sem, ytr_sem, yss_sem, ysr_sem, yas_sem, yar_sem, xs_sem, xr_sem, ts_sem, tr_sem,
):
    me = lax.axis_index("expert")
    dp = lax.axis_index("dp")
    tokens, width = tok.shape
    hidden = wg.shape[1]
    slots = experts * capp
    levels = replicas.bit_length() - 1
    half = width // 2
    bits = [lax.rem(dp // (1 << b), 2) for b in range(levels)]
    mates = [dp + (1 << b) * (1 - 2 * bits[b]) for b in range(levels)]
    top = levels - 1
    order = sorted(range(1, experts), key=lambda i: abs(2 * i - experts))

    def block(index):
        return pl.ds(pl.multiple_of(index * capp, capp), capp)

    loads = [
        pltpu.make_async_copy(src.at[0], dst, w_sem.at[j])
        for j, (src, dst) in enumerate(((wg_hbm, wg), (wu_hbm, wu), (wd_hbm, wd)))
    ]
    for load in loads:
        load.start()

    barrier = pltpu.get_barrier_semaphore()
    for i in range(1, experts):
        pl.semaphore_signal(
            barrier, inc=1, device_id={"expert": lax.rem(me + i, experts)}, device_id_type=MESH
        )
    for mate in mates:
        pl.semaphore_signal(barrier, inc=1, device_id={"dp": mate}, device_id_type=MESH)

    first, second = rout_t[0:1, :], rout_t[1:2, :]
    names = lax.broadcasted_iota(i32, ranks.shape, 0)
    is_first, is_second = names == first, names == second
    member = jnp.where(is_first | is_second, 1.0, 0.0).astype(f32)
    earlier = lax.broadcasted_iota(i32, (tokens, tokens), 0)
    later = lax.broadcasted_iota(i32, (tokens, tokens), 1)
    before = dot(member.astype(bf16), jnp.where(earlier < later, 1.0, 0.0).astype(bf16))
    ranks[...] = jnp.where(member > 0.0, before, -1.0).astype(i32)
    weights[...] = jnp.where(
        is_first, prob_t[0:1, :], jnp.where(is_second, prob_t[1:2, :], 0.0)
    )
    slot = lax.broadcasted_iota(i32, (capp, tokens), 0)

    def picks(expert):
        return slot == ranks[pl.ds(expert, 1), :]

    pl.semaphore_wait(barrier, experts - 1 + levels)

    tok_copies, cot_copies = [], []
    for i in order:
        k = lax.rem(me + i, experts)
        chosen = jnp.where(picks(k), 1.0, 0.0).astype(bf16)
        select[block(k), :] = chosen
        send_tok[block(k), :] = dot(chosen, tok[...]).astype(bf16)
        copy = pltpu.make_async_remote_copy(
            send_tok.at[block(k)], routed.at[block(me)], st_sem.at[i], rt_sem.at[i],
            device_id={"expert": k}, device_id_type=MESH,
        )
        copy.start()
        tok_copies.append(copy)

    def fill_cot(target, k):
        picked = picks(k)
        chosen = jnp.where(picked, 1.0, 0.0).astype(bf16)
        weight = jnp.sum(
            jnp.where(picked, weights[pl.ds(k, 1), :], 0.0), axis=1, keepdims=True
        )
        target[block(k), 0:width] = dot(chosen, cot[...]).astype(bf16)
        target[block(k), width:] = jnp.broadcast_to(weight, (capp, LANES)).astype(bf16)
        return chosen

    for i in order:
        k = lax.rem(me + i, experts)
        fill_cot(send_cot, k)
        copy = pltpu.make_async_remote_copy(
            send_cot.at[block(k)], cotp.at[block(me)], sc_sem.at[i], rc_sem.at[i],
            device_id={"expert": k}, device_id_type=MESH,
        )
        copy.start()
        cot_copies.append(copy)
    mine = fill_cot(cotp, me)
    select[block(me), :] = mine
    routed[block(me), :] = dot(mine, tok[...]).astype(bf16)

    kept_at = pl.multiple_of(bits[top] * half, LANES)
    handed_at = pl.multiple_of((1 - bits[top]) * half, LANES)
    y_copies = []

    def to_mate(source, target, send_sem, recv_sem):
        copy = pltpu.make_async_remote_copy(
            source, target, send_sem, recv_sem, device_id={"dp": mates[top]}, device_id_type=MESH
        )
        copy.start()
        y_copies.append(copy)
        return copy

    tok_to_mate, sca_to_mate, act_to_mate = [], [], {}
    for position, i in enumerate([0] + order):
        k = lax.rem(me + experts - i, experts)
        if i:
            tok_copies[position - 1].wait_recv()
        tok_to_mate.append(to_mate(
            routed.at[block(k), pl.ds(handed_at, half)], p_routed.at[block(k)],
            yts_sem.at[i], ytr_sem.at[i],
        ))

    loads[0].wait()
    loads[1].wait()

    @pl.loop(0, slots // ROWS)
    def _(step):
        rows = pl.ds(pl.multiple_of(step * ROWS, ROWS), ROWS)
        x = routed[rows, :]
        g = dot(x, wg[...])
        u = dot(x, wu[...])
        gate_pre[rows, :] = g
        up_pre[rows, :] = u
        acts[2, rows, :] = (g * jax.nn.sigmoid(g) * u).astype(bf16)

    def send_act(j):
        act_to_mate[j] = to_mate(acts.at[j], p_acts.at[j], yas_sem.at[j], yar_sem.at[j])

    send_act(2)

    for position, i in enumerate([0] + order):
        k = lax.rem(me + experts - i, experts)
        if i:
            cot_copies[position - 1].wait_recv()
        weight = cotp[block(k), width:].astype(f32)[:, 0:1]
        scaled[block(k), :] = (weight * cotp[block(k), 0:width].astype(f32)).astype(bf16)
        sca_to_mate.append(to_mate(
            scaled.at[block(k), pl.ds(handed_at, half)], p_scaled.at[block(k)],
            yss_sem.at[i], ysr_sem.at[i],
        ))

    loads[2].wait()

    @pl.loop(0, slots // ROWS)
    def _(step):
        rows = pl.ds(pl.multiple_of(step * ROWS, ROWS), ROWS)
        hg = dot(scaled[rows, :], wd[...], 1, 1)
        g, u = gate_pre[rows, :], up_pre[rows, :]
        s = jax.nn.sigmoid(g)
        acts[1, rows, :] = (hg * (g * s)).astype(bf16)
        acts[0, rows, :] = (hg * u * s * (1.0 + g * (1.0 - s))).astype(bf16)

    send_act(1)
    send_act(0)

    scaling = 1.0 / (experts * cap)
    tot_rows = lax.broadcasted_iota(i32, (8, LANES), 0)

    def steps_of(level):
        return level + 1

    def step_at(grad, level, step):
        return grad * (levels * (levels + 1) // 2) + level * (level + 1) // 2 + step

    tot_copies, x_copies = [], []

    def share(grad, level, step):
        at = step_at(grad, level, step)
        bit = levels - 1 - level + step
        copy = pltpu.make_async_remote_copy(
            tot_send.at[at], tot_recv.at[at], ts_sem.at[at], tr_sem.at[at],
            device_id={"dp": mates[bit]}, device_id_type=MESH,
        )
        copy.start()
        tot_copies.append(copy)
        return copy

    def begin_totals(grad, level, own_sq, part_sq, inner):
        is_former = bits[levels - 1 - level] == 0
        former = jnp.where(is_former, own_sq, part_sq)
        latter = jnp.where(is_former, part_sq, own_sq)
        packed = jnp.where(
            tot_rows == 0, former, jnp.where(tot_rows == 1, latter, inner)
        )
        tot_send[step_at(grad, level, 0)] = packed
        return share(grad, level, 0)

    def end_totals(grad, level, copy):
        for step in range(steps_of(level)):
            at = step_at(grad, level, step)
            copy.wait_recv()
            total = tot_send[at] + tot_recv[at]
            if step + 1 < steps_of(level):
                tot_send[at + 1] = total
                copy = share(grad, level, step + 1)
        former, latter, inner = total[0:1, 0:1], total[1:2, 0:1], total[2:3, 0:1]
        former_coef = 1.0 - inner / (2.0 * (former + epsilon))
        latter_coef = 1.0 - inner / (2.0 * (latter + epsilon))
        is_former = bits[levels - 1 - level] == 0
        return (
            jnp.where(is_former, former_coef, latter_coef),
            jnp.where(is_former, latter_coef, former_coef),
        )

    def whole(partial):
        return jnp.sum(partial, axis=1, keepdims=True)

    def first_level(grad):
        left, p_left = (scaled, p_scaled) if grad == 2 else (routed, p_routed)
        zero = jnp.zeros((1, hidden), f32)

        def body(step, sums):
            here = pl.multiple_of(step * LANES, LANES)
            there = pl.multiple_of(kept_at + step * LANES, LANES)
            a = dot(left[:, pl.ds(there, LANES)], acts[grad], 0, 0) * scaling
            b = dot(p_left[:, pl.ds(here, LANES)], p_acts[grad], 0, 0) * scaling
            own[grad, pl.ds(here, LANES), :] = a
            part[grad, pl.ds(here, LANES), :] = b
            return (
                sums[0] + jnp.sum(a * a, axis=0, keepdims=True),
                sums[1] + jnp.sum(b * b, axis=0, keepdims=True),
                sums[2] + jnp.sum(a * b, axis=0, keepdims=True),
            )

        sums = lax.fori_loop(0, half // LANES, body, (zero, zero, zero))
        return begin_totals(grad, 0, *[whole(s) for s in sums])

    def x_at(grad, level):
        return grad * max(levels - 1, 1) + level - 1

    def hand_over(grad, level, coefs):
        bit = levels - 1 - level
        size = half >> level
        keep_from = pl.multiple_of(bits[bit] * size, LANES)
        hand_from = pl.multiple_of((1 - bits[bit]) * size, LANES)
        sent = handed.at[grad, pl.ds(half - (half >> (level - 1)), size), :]
        at = x_at(grad, level)

        @pl.loop(0, size // LANES)
        def _(step):
            here = pl.multiple_of(step * LANES, LANES)
            theirs = pl.ds(pl.multiple_of(hand_from + step * LANES, LANES), LANES)
            sent[pl.ds(here, LANES), :] = (
                coefs[0] * own[grad, theirs, :] + coefs[1] * part[grad, theirs, :]
            ).astype(bf16)

        copy = pltpu.make_async_remote_copy(
            sent, landed.at[grad, pl.ds(half - (half >> (level - 1)), size), :],
            xs_sem.at[at], xr_sem.at[at], device_id={"dp": mates[bit]}, device_id_type=MESH,
        )
        copy.start()
        x_copies.append(copy)

        @pl.loop(0, size // LANES)
        def _(step):
            here = pl.multiple_of(step * LANES, LANES)
            ours = pl.ds(pl.multiple_of(keep_from + step * LANES, LANES), LANES)
            own[grad, pl.ds(here, LANES), :] = (
                coefs[0] * own[grad, ours, :] + coefs[1] * part[grad, ours, :]
            )

        return copy

    def next_level(grad, level, copy):
        size = half >> level
        start = half - (half >> (level - 1))
        copy.wait_recv()
        zero = jnp.zeros((1, hidden), f32)

        def body(step, sums):
            here = pl.ds(pl.multiple_of(step * LANES, LANES), LANES)
            a = own[grad, here, :]
            b = landed[grad, pl.ds(pl.multiple_of(start + step * LANES, LANES), LANES), :]
            b = b.astype(f32)
            part[grad, here, :] = b
            return (
                sums[0] + jnp.sum(a * a, axis=0, keepdims=True),
                sums[1] + jnp.sum(b * b, axis=0, keepdims=True),
                sums[2] + jnp.sum(a * b, axis=0, keepdims=True),
            )

        sums = lax.fori_loop(0, size // LANES, body, (zero, zero, zero))
        return begin_totals(grad, level, *[whole(s) for s in sums])

    def finish(grad, coefs):
        size = half >> (levels - 1)
        target = (out_gate, out_up, out_down)[grad]

        @pl.loop(0, size // LANES)
        def _(step):
            here = pl.ds(pl.multiple_of(step * LANES, LANES), LANES)
            value = coefs[0] * own[grad, here, :] + coefs[1] * part[grad, here, :]
            if grad == 2:
                target[0, :, here] = value.T
            else:
                target[0, here, :] = value

    for copy in sca_to_mate + tok_to_mate:
        copy.wait_recv()
    act_to_mate[2].wait_recv()
    pending = {2: first_level(2)}

    @pl.loop(0, slots // ROWS)
    def _(step):
        rows = pl.ds(pl.multiple_of(step * ROWS, ROWS), ROWS)
        back = dot(acts[0, rows, :], wg[...], 1, 1) + dot(acts[1, rows, :], wu[...], 1, 1)
        ret_send[rows, 0:width] = back.astype(bf16)
        output = dot(acts[2, rows, :], wd[...])
        score = jnp.sum(output * cotp[rows, 0:width].astype(f32), axis=1, keepdims=True)
        ret_send[rows, width:] = jnp.broadcast_to(score, (ROWS, LANES)).astype(bf16)

    ret_copies = []
    for i in order:
        k = lax.rem(me + i, experts)
        copy = pltpu.make_async_remote_copy(
            ret_send.at[block(k)], ret_recv.at[block(me)], sr_sem.at[i], rr_sem.at[i],
            device_id={"expert": k}, device_id_type=MESH,
        )
        copy.start()
        ret_copies.append(copy)
    ret_recv[block(me), :] = ret_send[block(me), :]

    moving = {}
    for grad in (2, 1, 0):
        if grad != 2:
            act_to_mate[grad].wait_recv()
            pending[grad] = first_level(grad)
        coefs = end_totals(grad, 0, pending[grad])
        if levels > 1:
            moving[grad] = hand_over(grad, 1, coefs)
        else:
            finish(grad, coefs)
    for level in range(1, levels):
        for grad in (2, 1, 0):
            pending[grad] = next_level(grad, level, moving[grad])
            coefs = end_totals(grad, level, pending[grad])
            if level + 1 < levels:
                moving[grad] = hand_over(grad, level + 1, coefs)
            else:
                finish(grad, coefs)

    for copy in ret_copies:
        copy.wait_recv()

    @pl.loop(0, width // 512)
    def _(step):
        columns = pl.ds(pl.multiple_of(step * 512, 512), 512)
        out_in[:, columns] = dot(select[...], ret_recv[:, columns], 0, 0).astype(bf16)

    chosen_by = rout[...]
    scores = jnp.zeros((tokens, chosen_by.shape[1]), f32)
    for k in range(experts):
        rows = slice(k * capp, (k + 1) * capp)
        score = dot(select[rows, :], ret_recv[rows, width:], 0, 0)
        scores = scores + jnp.where(chosen_by == k, score[:, 0 : chosen_by.shape[1]], 0.0)
    out_router[...] = scores.astype(bf16)

    for copy in tok_copies + cot_copies + ret_copies + y_copies + tot_copies + x_copies:
        copy.wait_send()


def kernel(
    experts, replicas, cap, capp,
    tok, cot, rout, rout_t, prob_t, wg_hbm, wu_hbm, wd_hbm,
    out_gate, out_up, out_down, out_in, out_router,
    wg, wu, wd, ranks, weights, select, send_tok, send_cot, got_tok, got_cot, routed, cotp, scaled,
    gate_pre, up_pre, acts, p_routed, p_scaled, p_acts, ret_send, ret_recv,
    grads, gram_send, gram_recv,
    w_sem, st_sem, rt_sem, sc_sem, rc_sem, sr_sem, rr_sem,
    yts_sem, ytr_sem, yss_sem, ysr_sem, yas_sem, yar_sem, gs_sem, gr_sem, kts_sem, ktr_sem, kcs_sem, kcr_sem,
):
    me = lax.axis_index("expert")
    dp = lax.axis_index("dp")
    tokens, width = tok.shape
    hidden = wg.shape[1]
    slots = experts * capp
    levels = replicas.bit_length() - 1
    quarter = width // replicas
    bits = [lax.rem(dp // (1 << b), 2) for b in range(levels)]
    mates = [
        dp + sum((1 << b) * (1 - 2 * bits[b]) for b in range(levels) if j >> b & 1)
        for j in range(replicas)
    ]
    others = range(1, replicas)
    order = sorted(range(1, experts), key=lambda i: abs(2 * i - experts))
    chips = experts // 2
    here_chip, core = me // 2, lax.rem(me, 2)
    sibling = me + 1 - 2 * core
    both = -(-2 * cap // 16) * 16
    offset, shift = cap // 16 * 16, cap % 16
    chip_order = sorted(range(1, chips), key=lambda i: abs(2 * i - chips))

    def block(index):
        return pl.ds(pl.multiple_of(index * capp, capp), capp)

    loads = [
        pltpu.make_async_copy(src.at[0], dst, w_sem.at[j])
        for j, (src, dst) in enumerate(((wg_hbm, wg), (wu_hbm, wu), (wd_hbm, wd)))
    ]
    for load in loads:
        load.start()

    barrier = pltpu.get_barrier_semaphore()
    for i in range(1, experts):
        pl.semaphore_signal(
            barrier, inc=1, device_id={"expert": lax.rem(me + i, experts)}, device_id_type=MESH
        )
    for mate in mates[1:]:
        pl.semaphore_signal(barrier, inc=1, device_id={"dp": mate}, device_id_type=MESH)

    first, second = rout_t[0:1, :], rout_t[1:2, :]
    names = lax.broadcasted_iota(i32, ranks.shape, 0)
    is_first, is_second = names == first, names == second
    member = jnp.where(is_first | is_second, 1.0, 0.0).astype(f32)
    earlier = lax.broadcasted_iota(i32, (tokens, tokens), 0)
    later = lax.broadcasted_iota(i32, (tokens, tokens), 1)
    before = dot(member.astype(bf16), jnp.where(earlier < later, 1.0, 0.0).astype(bf16))
    ranks[...] = jnp.where(member > 0.0, before, -1024.0).astype(i32)
    weights[...] = jnp.where(
        is_first, prob_t[0:1, :], jnp.where(is_second, prob_t[1:2, :], 0.0)
    )
    slot = lax.broadcasted_iota(i32, (capp, tokens), 0)
    both_slot = lax.broadcasted_iota(i32, (both, tokens), 0)

    def pair(chip):
        return pl.ds(pl.multiple_of(chip * both, 16), both)

    def window(chip, which):
        return pl.ds(pl.multiple_of(chip * both + which * offset, 16), capp)

    def fill_tok(target, chip):
        low = both_slot == ranks[pl.ds(2 * chip, 1), :]
        high = both_slot == cap + ranks[pl.ds(2 * chip + 1, 1), :]
        chosen = jnp.where(low | high, 1.0, 0.0).astype(bf16)
        target[pair(chip), :] = dot(chosen, tok[...]).astype(bf16)

    def fill_cot(target, chip):
        low = both_slot == ranks[pl.ds(2 * chip, 1), :]
        high = both_slot == cap + ranks[pl.ds(2 * chip + 1, 1), :]
        chosen = jnp.where(low | high, 1.0, 0.0).astype(bf16)
        held = jnp.where(low, weights[pl.ds(2 * chip, 1), :], 0.0)
        held = jnp.where(high, weights[pl.ds(2 * chip + 1, 1), :], held)
        weight = jnp.sum(held, axis=1, keepdims=True)
        target[pair(chip), 0:width] = dot(chosen, cot[...]).astype(bf16)
        target[pair(chip), width:] = jnp.broadcast_to(weight, (both, LANES)).astype(bf16)

    pl.semaphore_wait(barrier, experts + replicas - 2)

    tok_copies, cot_copies = [], []
    def to_chip(i, source, target, send_sem, recv_sem):
        chip = lax.rem(here_chip + i, chips)
        copy = pltpu.make_async_remote_copy(
            source.at[pair(chip)], target.at[pair(here_chip)], send_sem.at[i], recv_sem.at[i],
            device_id={"expert": 2 * chip + core}, device_id_type=MESH,
        )
        copy.start()
        return copy

    for i in chip_order:
        fill_tok(send_tok, lax.rem(here_chip + i, chips))
        tok_copies.append(to_chip(i, send_tok, got_tok, st_sem, rt_sem))
    for i in chip_order:
        fill_cot(send_cot, lax.rem(here_chip + i, chips))
        cot_copies.append(to_chip(i, send_cot, got_cot, sc_sem, rc_sem))
    fill_tok(got_tok, here_chip)
    fill_cot(got_cot, here_chip)
    for k in range(experts):
        picked = slot == ranks[k : k + 1, :] + k % 2 * shift
        select[k * capp : (k + 1) * capp, :] = jnp.where(picked, 1.0, 0.0).astype(bf16)

    core_copies = []

    def to_sibling(chip, i, source, target, send_sem, recv_sem):
        copy = pltpu.make_async_remote_copy(
            source.at[window(chip, 1 - core)], target.at[block(2 * chip + core)],
            send_sem.at[i], recv_sem.at[i], device_id={"expert": sibling}, device_id_type=MESH,
        )
        copy.start()
        core_copies.append(copy)
        return copy

    y_copies = []

    def columns_of(mate):
        return pl.ds(pl.multiple_of(mate * quarter, LANES), quarter)

    def to_mate(j, source, target, send_sem, recv_sem):
        copy = pltpu.make_async_remote_copy(
            source, target, send_sem, recv_sem, device_id={"dp": mates[j]}, device_id_type=MESH
        )
        copy.start()
        y_copies.append(copy)
        return copy

    tok_to_mate, sca_to_mate, act_to_mate = [], [], {}
    def spread_tok(which, i):
        for j in others:
            tok_to_mate.append(to_mate(
                j, routed.at[block(which), columns_of(mates[j])], p_routed.at[j, block(which)],
                yts_sem.at[j, i], ytr_sem.at[j, i],
            ))

    def from_sibling(chip, i, copy):
        copy.wait_recv()
        spread_tok(2 * chip + 1 - core, 2 * i + 1)

    last = None
    for position, i in enumerate([0] + chip_order):
        chip = lax.rem(here_chip + chips - i, chips)
        if i:
            tok_copies[position - 1].wait_recv()
        copy = to_sibling(chip, i, got_tok, routed, kts_sem, ktr_sem)
        routed[block(2 * chip + core), :] = got_tok[window(chip, core), :]
        if last:
            from_sibling(*last)
        spread_tok(2 * chip + core, 2 * i)
        last = (chip, i, copy)
    from_sibling(*last)

    loads[0].wait()
    loads[1].wait()

    @pl.loop(0, slots // ROWS)
    def _(step):
        rows = pl.ds(pl.multiple_of(step * ROWS, ROWS), ROWS)
        x = routed[rows, :]
        g = dot(x, wg[...])
        u = dot(x, wu[...])
        gate_pre[rows, :] = g
        up_pre[rows, :] = u
        acts[2, rows, :] = (g * jax.nn.sigmoid(g) * u).astype(bf16)

    def send_act(grad, j, source=None):
        act_to_mate[grad, source or j] = to_mate(
            j, p_acts.at[grad, source ^ j] if source else acts.at[grad],
            p_acts.at[grad, source or j],
            yas_sem.at[grad, source or j], yar_sem.at[grad, source or j],
        )

    for j in others:
        send_act(2, j)

    line = lax.broadcasted_iota(i32, (capp, 1), 0)
    valid = (line >= core * shift) & (line < core * shift + cap)

    def spread_cot(which, i):
        weight = jnp.where(valid, cotp[block(which), width:].astype(f32)[:, 0:1], 0.0)
        scaled[block(which), :] = (
            weight * cotp[block(which), 0:width].astype(f32)
        ).astype(bf16)
        for j in others:
            sca_to_mate.append(to_mate(
                j, scaled.at[block(which), columns_of(mates[j])], p_scaled.at[j, block(which)],
                yss_sem.at[j, i], ysr_sem.at[j, i],
            ))

    def cot_from_sibling(chip, i, copy):
        copy.wait_recv()
        spread_cot(2 * chip + 1 - core, 2 * i + 1)

    last = None
    for position, i in enumerate([0] + chip_order):
        chip = lax.rem(here_chip + chips - i, chips)
        if i:
            cot_copies[position - 1].wait_recv()
        copy = to_sibling(chip, i, got_cot, cotp, kcs_sem, kcr_sem)
        cotp[block(2 * chip + core), :] = got_cot[window(chip, core), :]
        if last:
            cot_from_sibling(*last)
        spread_cot(2 * chip + core, 2 * i)
        last = (chip, i, copy)
    cot_from_sibling(*last)

    loads[2].wait()

    @pl.loop(0, slots // ROWS)
    def _(step):
        rows = pl.ds(pl.multiple_of(step * ROWS, ROWS), ROWS)
        hg = dot(scaled[rows, :], wd[...], 1, 1)
        g, u = gate_pre[rows, :], up_pre[rows, :]
        s = jax.nn.sigmoid(g)
        acts[1, rows, :] = (hg * (g * s)).astype(bf16)
        acts[0, rows, :] = (hg * u * s * (1.0 + g * (1.0 - s))).astype(bf16)

    relayed = replicas == 4
    near = (1, 2) if relayed else others
    for grad in (1, 0):
        for j in near:
            send_act(grad, j)

    scaling = 1.0 / (experts * cap)
    pairs = [(i, j) for i in range(replicas) for j in range(i, replicas)]

    def grad_of(grad, j):
        left, p_left = (scaled, p_scaled) if grad == 2 else (routed, p_routed)

        @pl.loop(0, quarter // LANES)
        def _(step):
            here = pl.ds(pl.multiple_of(step * LANES, LANES), LANES)
            if j:
                x, y = p_left[j, :, here], p_acts[grad, j]
            else:
                there = pl.multiple_of(dp * quarter + step * LANES, LANES)
                x, y = left[:, pl.ds(there, LANES)], acts[grad]
            grads[grad, j, here, :] = dot(x, y, 0, 0) * scaling

    def gram_of(grad):
        def body(step, sums):
            here = pl.ds(pl.multiple_of(step * 8, 8), 8)
            held = [grads[grad, j, here, :] for j in range(replicas)]
            return tuple(s + held[i] * held[j] for s, (i, j) in zip(sums, pairs))

        zero = jnp.zeros((8, hidden), f32)
        sums = lax.fori_loop(0, quarter // 8, body, (zero,) * len(pairs))
        for row, total in enumerate(sums):
            total = jnp.sum(jnp.sum(total, axis=0, keepdims=True), axis=1, keepdims=True)
            gram_send[grad, row : row + 1, :] = jnp.broadcast_to(total, (1, LANES))

    def combine(grad):
        def entry(i, j):
            total = 0.0
            for m in range(replicas):
                row = pairs.index(tuple(sorted((i ^ m, j ^ m))))
                held = gram_recv[m, grad, row : row + 1, :] if m else gram_send[grad, row : row + 1, :]
                total = total + held
            return total

        gram = {pair: entry(*pair) for pair in pairs}

        def product(left, right):
            return sum(
                left[i] * right[j] * gram[min(i, j), max(i, j)] for i in left for j in right
            )

        vectors = [{j: jnp.ones((1, LANES), f32)} for j in range(replicas)]
        while len(vectors) > 1:
            count = len(vectors) // 2
            joined = []
            for j in range(count):
                a, b = vectors[j], vectors[j + count]
                inner = product(a, b)
                na = jnp.maximum(product(a, a), 0.0)
                nb = jnp.maximum(product(b, b), 0.0)
                ca = 1.0 - inner / (2.0 * (na + epsilon))
                cb = 1.0 - inner / (2.0 * (nb + epsilon))
                joined.append({
                    **{i: ca * c for i, c in a.items()}, **{i: cb * c for i, c in b.items()}
                })
            vectors = joined
        coefs = [vectors[0][j][:, 0:1] for j in range(replicas)]
        target = (out_gate, out_up, out_down)[grad]

        @pl.loop(0, quarter // LANES)
        def _(step):
            here = pl.ds(pl.multiple_of(step * LANES, LANES), LANES)
            value = coefs[0] * grads[grad, 0, here, :]
            for j in others:
                value = value + coefs[j] * grads[grad, j, here, :]
            if grad == 2:
                target[0, :, here] = value.T
            else:
                target[0, here, :] = value

    @pl.loop(0, slots // ROWS)
    def _(step):
        rows = pl.ds(pl.multiple_of(step * ROWS, ROWS), ROWS)
        back = dot(acts[0, rows, :], wg[...], 1, 1) + dot(acts[1, rows, :], wu[...], 1, 1)
        ret_send[rows, 0:width] = back.astype(bf16)
        output = dot(acts[2, rows, :], wd[...])
        score = jnp.sum(output * cotp[rows, 0:width].astype(f32), axis=1, keepdims=True)
        ret_send[rows, width:] = jnp.broadcast_to(score, (ROWS, LANES)).astype(bf16)

    ret_copies = []
    for i in order:
        k = lax.rem(me + i, experts)
        copy = pltpu.make_async_remote_copy(
            ret_send.at[block(k)], ret_recv.at[block(me)], sr_sem.at[i], rr_sem.at[i],
            device_id={"expert": k}, device_id_type=MESH,
        )
        copy.start()
        ret_copies.append(copy)
    ret_recv[block(me), :] = ret_send[block(me), :]

    for copy in sca_to_mate + tok_to_mate:
        copy.wait_recv()
    for grad in (2, 1, 0):
        grad_of(grad, 0)
    for j in others:
        act_to_mate[2, j].wait_recv()
        grad_of(2, j)
    gram_of(2)
    for grad, far in ((1, 1), (0, 2)):
        for j in near:
            act_to_mate[grad, j].wait_recv()
        if relayed:
            send_act(grad, far, 3)
        for j in near:
            grad_of(grad, j)
    for grad in (1, 0):
        if relayed:
            act_to_mate[grad, 3].wait_recv()
            grad_of(grad, 3)
        gram_of(grad)
    gram_copies = []
    for j in others:
        copy = pltpu.make_async_remote_copy(
            gram_send, gram_recv.at[j], gs_sem.at[j], gr_sem.at[j],
            device_id={"dp": mates[j]}, device_id_type=MESH,
        )
        copy.start()
        gram_copies.append(copy)
    for copy in gram_copies:
        copy.wait_recv()
    for grad in (2, 1, 0):
        combine(grad)

    for copy in ret_copies:
        copy.wait_recv()

    @pl.loop(0, width // 512)
    def _(step):
        columns = pl.ds(pl.multiple_of(step * 512, 512), 512)
        out_in[:, columns] = dot(select[...], ret_recv[:, columns], 0, 0).astype(bf16)

    chosen_by = rout[...]
    scores = jnp.zeros((tokens, chosen_by.shape[1]), f32)
    for k in range(experts):
        rows = slice(k * capp, (k + 1) * capp)
        score = dot(select[rows, :], ret_recv[rows, width:], 0, 0)
        scores = scores + jnp.where(chosen_by == k, score[:, 0 : chosen_by.shape[1]], 0.0)
    out_router[...] = scores.astype(bf16)

    for copy in tok_copies + cot_copies + ret_copies + y_copies + gram_copies + core_copies:
        copy.wait_send()


def per_device(experts, replicas, tokens, routing, probs, cotangent, w_gate, w_up, w_down):
    rows, top = routing.shape
    width = tokens.shape[1]
    hidden = w_gate.shape[2]
    cap = 5 * rows * top // (4 * experts)
    capp = -(-cap // 16) * 16
    slots = experts * capp
    levels = replicas.bit_length() - 1
    half = width // 2
    shard = width // replicas
    direct = replicas <= 4
    steps = 3 * (levels * (levels + 1) // 2)
    wide = width + LANES
    vm, dma = pltpu.VMEM, pltpu.SemaphoreType.DMA
    in_vmem = pl.BlockSpec(memory_space=pltpu.VMEM)
    in_any = pl.BlockSpec(memory_space=pl.ANY)
    paired = experts // 2 * (-(-2 * cap // 16) * 16)
    names = max(16, experts)
    grams = -(-replicas * (replicas + 1) // 16) * 8
    return tuple(pl.pallas_call(
        functools.partial(kernel if direct else halving_kernel, experts, replicas, cap, capp),
        out_shape=(
            jax.ShapeDtypeStruct((1, shard, hidden), f32),
            jax.ShapeDtypeStruct((1, shard, hidden), f32),
            jax.ShapeDtypeStruct((1, hidden, shard), f32),
            jax.ShapeDtypeStruct((rows, width), bf16),
            jax.ShapeDtypeStruct((rows, top), bf16),
        ),
        in_specs=[in_vmem] * 5 + [in_any] * 3,
        out_specs=(in_vmem,) * 5,
        scratch_shapes=[
            vm((width, hidden), bf16), vm((width, hidden), bf16), vm((hidden, width), bf16),
            vm((names, rows), i32), vm((names, rows), f32), vm((slots, rows), bf16),
        ] + ([
            vm((paired, width), bf16), vm((paired, wide), bf16),
            vm((paired, width), bf16), vm((paired, wide), bf16),
        ] if direct else [
            vm((slots, width), bf16), vm((slots, wide), bf16),
        ]) + [
            vm((slots, width), bf16), vm((slots, wide), bf16), vm((slots, width), bf16),
            vm((slots, hidden), f32), vm((slots, hidden), f32), vm((3, slots, hidden), bf16),
        ] + ([
            vm((replicas, slots, shard), bf16), vm((replicas, slots, shard), bf16),
            vm((3, replicas, slots, hidden), bf16),
        ] if direct else [
            vm((slots, half), bf16), vm((slots, half), bf16), vm((3, slots, hidden), bf16),
        ]) + [
            vm((slots, wide), bf16), vm((slots, wide), bf16),
        ] + ([
            vm((3, replicas, shard, hidden), f32),
            vm((3, grams, LANES), f32), vm((replicas, 3, grams, LANES), f32),
        ] if direct else [
            vm((3, half, hidden), f32), vm((3, half, hidden), f32),
            vm((3, half, hidden), bf16), vm((3, half, hidden), bf16),
            vm((steps, 8, LANES), f32), vm((steps, 8, LANES), f32),
        ]) + [dma((3,))] + [dma((experts,))] * 6 + ([
            dma((replicas, experts)), dma((replicas, experts)),
            dma((replicas, experts)), dma((replicas, experts)),
            dma((3, replicas)), dma((3, replicas)), dma((replicas,)), dma((replicas,)),
            dma((experts // 2,)), dma((experts // 2,)), dma((experts // 2,)), dma((experts // 2,)),
        ] if direct else [dma((experts,))] * 4 + [dma((3,))] * 2
            + [dma((3 * max(levels - 1, 1),))] * 2 + [dma((steps,))] * 2),
        compiler_params=pltpu.CompilerParams(
            collective_id=0, has_side_effects=True, vmem_limit_bytes=67_000_000
        ),
        name="adasum_moe",
    )(
        tokens, cotangent, routing, routing.T, probs.T.astype(f32), w_gate, w_up, w_down
    ))


def solution(mesh):
    rows = P(("dp", "expert"), None)
    return jax.shard_map(
        functools.partial(per_device, mesh.shape["expert"], mesh.shape["dp"]),
        mesh=mesh,
        in_specs=(rows,) * 4 + (P("expert", None, None),) * 3,
        out_specs=(
            P("expert", "dp", None),
            P("expert", "dp", None),
            P("expert", None, "dp"),
            rows,
            rows,
        ),
        check_vma=False,
    )
```

```python
import functools

import jax
import jax.numpy as jnp
from jax import lax
from jax.experimental import pallas as pl
from jax.experimental.pallas import tpu as pltpu
from jax.sharding import PartitionSpec as P

epsilon = 1e-06
MESH = pl.DeviceIdType.MESH
f32, bf16, i32 = jnp.float32, jnp.bfloat16, jnp.int32
ROWS = 128
LANES = 128


def dot(a, b, ad=1, bd=0):
    return lax.dot_general(a, b, (((ad,), (bd,)), ((), ())), preferred_element_type=f32)


def halving_kernel(
    experts, replicas, cap, capp,
    tok, cot, rout, rout_t, prob_t, wg_hbm, wu_hbm, wd_hbm,
    out_gate, out_up, out_down, out_in, out_router,
    wg, wu, wd, ranks, weights, select, send_tok, send_cot, routed, cotp, scaled,
    gate_pre, up_pre, acts, p_routed, p_scaled, p_acts, ret_send, ret_recv,
    own, part, handed, landed, tot_send, tot_recv,
    w_sem, st_sem, rt_sem, sc_sem, rc_sem, sr_sem, rr_sem,
    yts_sem, ytr_sem, yss_sem, ysr_sem, yas_sem, yar_sem, xs_sem, xr_sem, ts_sem, tr_sem,
):
    me = lax.axis_index("expert")
    dp = lax.axis_index("dp")
    tokens, width = tok.shape
    hidden = wg.shape[1]
    slots = experts * capp
    levels = replicas.bit_length() - 1
    half = width // 2
    bits = [lax.rem(dp // (1 << b), 2) for b in range(levels)]
    mates = [dp + (1 << b) * (1 - 2 * bits[b]) for b in range(levels)]
    top = levels - 1
    order = sorted(range(1, experts), key=lambda i: abs(2 * i - experts))

    def block(index):
        return pl.ds(pl.multiple_of(index * capp, capp), capp)

    loads = [
        pltpu.make_async_copy(src.at[0], dst, w_sem.at[j])
        for j, (src, dst) in enumerate(((wg_hbm, wg), (wu_hbm, wu), (wd_hbm, wd)))
    ]
    for load in loads:
        load.start()

    barrier = pltpu.get_barrier_semaphore()
    for i in range(1, experts):
        pl.semaphore_signal(
            barrier, inc=1, device_id={"expert": lax.rem(me + i, experts)}, device_id_type=MESH
        )
    for mate in mates:
        pl.semaphore_signal(barrier, inc=1, device_id={"dp": mate}, device_id_type=MESH)

    first, second = rout_t[0:1, :], rout_t[1:2, :]
    names = lax.broadcasted_iota(i32, ranks.shape, 0)
    is_first, is_second = names == first, names == second
    member = jnp.where(is_first | is_second, 1.0, 0.0).astype(f32)
    earlier = lax.broadcasted_iota(i32, (tokens, tokens), 0)
    later = lax.broadcasted_iota(i32, (tokens, tokens), 1)
    before = dot(member.astype(bf16), jnp.where(earlier < later, 1.0, 0.0).astype(bf16))
    ranks[...] = jnp.where(member > 0.0, before, -1.0).astype(i32)
    weights[...] = jnp.where(
        is_first, prob_t[0:1, :], jnp.where(is_second, prob_t[1:2, :], 0.0)
    )
    slot = lax.broadcasted_iota(i32, (capp, tokens), 0)

    def picks(expert):
        return slot == ranks[pl.ds(expert, 1), :]

    pl.semaphore_wait(barrier, experts - 1 + levels)

    tok_copies, cot_copies = [], []
    for i in order:
        k = lax.rem(me + i, experts)
        chosen = jnp.where(picks(k), 1.0, 0.0).astype(bf16)
        select[block(k), :] = chosen
        send_tok[block(k), :] = dot(chosen, tok[...]).astype(bf16)
        copy = pltpu.make_async_remote_copy(
            send_tok.at[block(k)], routed.at[block(me)], st_sem.at[i], rt_sem.at[i],
            device_id={"expert": k}, device_id_type=MESH,
        )
        copy.start()
        tok_copies.append(copy)

    def fill_cot(target, k):
        picked = picks(k)
        chosen = jnp.where(picked, 1.0, 0.0).astype(bf16)
        weight = jnp.sum(
            jnp.where(picked, weights[pl.ds(k, 1), :], 0.0), axis=1, keepdims=True
        )
        target[block(k), 0:width] = dot(chosen, cot[...]).astype(bf16)
        target[block(k), width:] = jnp.broadcast_to(weight, (capp, LANES)).astype(bf16)
        return chosen

    for i in order:
        k = lax.rem(me + i, experts)
        fill_cot(send_cot, k)
        copy = pltpu.make_async_remote_copy(
            send_cot.at[block(k)], cotp.at[block(me)], sc_sem.at[i], rc_sem.at[i],
            device_id={"expert": k}, device_id_type=MESH,
        )
        copy.start()
        cot_copies.append(copy)
    mine = fill_cot(cotp, me)
    select[block(me), :] = mine
    routed[block(me), :] = dot(mine, tok[...]).astype(bf16)

    kept_at = pl.multiple_of(bits[top] * half, LANES)
    handed_at = pl.multiple_of((1 - bits[top]) * half, LANES)
    y_copies = []

    def to_mate(source, target, send_sem, recv_sem):
        copy = pltpu.make_async_remote_copy(
            source, target, send_sem, recv_sem, device_id={"dp": mates[top]}, device_id_type=MESH
        )
        copy.start()
        y_copies.append(copy)
        return copy

    tok_to_mate, sca_to_mate, act_to_mate = [], [], {}
    for position, i in enumerate([0] + order):
        k = lax.rem(me + experts - i, experts)
        if i:
            tok_copies[position - 1].wait_recv()
        tok_to_mate.append(to_mate(
            routed.at[block(k), pl.ds(handed_at, half)], p_routed.at[block(k)],
            yts_sem.at[i], ytr_sem.at[i],
        ))

    loads[0].wait()
    loads[1].wait()

    @pl.loop(0, slots // ROWS)
    def _(step):
        rows = pl.ds(pl.multiple_of(step * ROWS, ROWS), ROWS)
        x = routed[rows, :]
        g = dot(x, wg[...])
        u = dot(x, wu[...])
        gate_pre[rows, :] = g
        up_pre[rows, :] = u
        acts[2, rows, :] = (g * jax.nn.sigmoid(g) * u).astype(bf16)

    def send_act(j):
        act_to_mate[j] = to_mate(acts.at[j], p_acts.at[j], yas_sem.at[j], yar_sem.at[j])

    send_act(2)

    for position, i in enumerate([0] + order):
        k = lax.rem(me + experts - i, experts)
        if i:
            cot_copies[position - 1].wait_recv()
        weight = cotp[block(k), width:].astype(f32)[:, 0:1]
        scaled[block(k), :] = (weight * cotp[block(k), 0:width].astype(f32)).astype(bf16)
        sca_to_mate.append(to_mate(
            scaled.at[block(k), pl.ds(handed_at, half)], p_scaled.at[block(k)],
            yss_sem.at[i], ysr_sem.at[i],
        ))

    loads[2].wait()

    @pl.loop(0, slots // ROWS)
    def _(step):
        rows = pl.ds(pl.multiple_of(step * ROWS, ROWS), ROWS)
        hg = dot(scaled[rows, :], wd[...], 1, 1)
        g, u = gate_pre[rows, :], up_pre[rows, :]
        s = jax.nn.sigmoid(g)
        acts[1, rows, :] = (hg * (g * s)).astype(bf16)
        acts[0, rows, :] = (hg * u * s * (1.0 + g * (1.0 - s))).astype(bf16)

    send_act(1)
    send_act(0)

    scaling = 1.0 / (experts * cap)
    tot_rows = lax.broadcasted_iota(i32, (8, LANES), 0)

    def steps_of(level):
        return level + 1

    def step_at(grad, level, step):
        return grad * (levels * (levels + 1) // 2) + level * (level + 1) // 2 + step

    tot_copies, x_copies = [], []

    def share(grad, level, step):
        at = step_at(grad, level, step)
        bit = levels - 1 - level + step
        copy = pltpu.make_async_remote_copy(
            tot_send.at[at], tot_recv.at[at], ts_sem.at[at], tr_sem.at[at],
            device_id={"dp": mates[bit]}, device_id_type=MESH,
        )
        copy.start()
        tot_copies.append(copy)
        return copy

    def begin_totals(grad, level, own_sq, part_sq, inner):
        is_former = bits[levels - 1 - level] == 0
        former = jnp.where(is_former, own_sq, part_sq)
        latter = jnp.where(is_former, part_sq, own_sq)
        packed = jnp.where(
            tot_rows == 0, former, jnp.where(tot_rows == 1, latter, inner)
        )
        tot_send[step_at(grad, level, 0)] = packed
        return share(grad, level, 0)

    def end_totals(grad, level, copy):
        for step in range(steps_of(level)):
            at = step_at(grad, level, step)
            copy.wait_recv()
            total = tot_send[at] + tot_recv[at]
            if step + 1 < steps_of(level):
                tot_send[at + 1] = total
                copy = share(grad, level, step + 1)
        former, latter, inner = total[0:1, 0:1], total[1:2, 0:1], total[2:3, 0:1]
        former_coef = 1.0 - inner / (2.0 * (former + epsilon))
        latter_coef = 1.0 - inner / (2.0 * (latter + epsilon))
        is_former = bits[levels - 1 - level] == 0
        return (
            jnp.where(is_former, former_coef, latter_coef),
            jnp.where(is_former, latter_coef, former_coef),
        )

    def whole(partial):
        return jnp.sum(partial, axis=1, keepdims=True)

    def first_level(grad):
        left, p_left = (scaled, p_scaled) if grad == 2 else (routed, p_routed)
        zero = jnp.zeros((1, hidden), f32)

        def body(step, sums):
            here = pl.multiple_of(step * LANES, LANES)
            there = pl.multiple_of(kept_at + step * LANES, LANES)
            a = dot(left[:, pl.ds(there, LANES)], acts[grad], 0, 0) * scaling
            b = dot(p_left[:, pl.ds(here, LANES)], p_acts[grad], 0, 0) * scaling
            own[grad, pl.ds(here, LANES), :] = a
            part[grad, pl.ds(here, LANES), :] = b
            return (
                sums[0] + jnp.sum(a * a, axis=0, keepdims=True),
                sums[1] + jnp.sum(b * b, axis=0, keepdims=True),
                sums[2] + jnp.sum(a * b, axis=0, keepdims=True),
            )

        sums = lax.fori_loop(0, half // LANES, body, (zero, zero, zero))
        return begin_totals(grad, 0, *[whole(s) for s in sums])

    def x_at(grad, level):
        return grad * max(levels - 1, 1) + level - 1

    def hand_over(grad, level, coefs):
        bit = levels - 1 - level
        size = half >> level
        keep_from = pl.multiple_of(bits[bit] * size, LANES)
        hand_from = pl.multiple_of((1 - bits[bit]) * size, LANES)
        sent = handed.at[grad, pl.ds(half - (half >> (level - 1)), size), :]
        at = x_at(grad, level)

        @pl.loop(0, size // LANES)
        def _(step):
            here = pl.multiple_of(step * LANES, LANES)
            theirs = pl.ds(pl.multiple_of(hand_from + step * LANES, LANES), LANES)
            sent[pl.ds(here, LANES), :] = (
                coefs[0] * own[grad, theirs, :] + coefs[1] * part[grad, theirs, :]
            ).astype(bf16)

        copy = pltpu.make_async_remote_copy(
            sent, landed.at[grad, pl.ds(half - (half >> (level - 1)), size), :],
            xs_sem.at[at], xr_sem.at[at], device_id={"dp": mates[bit]}, device_id_type=MESH,
        )
        copy.start()
        x_copies.append(copy)

        @pl.loop(0, size // LANES)
        def _(step):
            here = pl.multiple_of(step * LANES, LANES)
            ours = pl.ds(pl.multiple_of(keep_from + step * LANES, LANES), LANES)
            own[grad, pl.ds(here, LANES), :] = (
                coefs[0] * own[grad, ours, :] + coefs[1] * part[grad, ours, :]
            )

        return copy

    def next_level(grad, level, copy):
        size = half >> level
        start = half - (half >> (level - 1))
        copy.wait_recv()
        zero = jnp.zeros((1, hidden), f32)

        def body(step, sums):
            here = pl.ds(pl.multiple_of(step * LANES, LANES), LANES)
            a = own[grad, here, :]
            b = landed[grad, pl.ds(pl.multiple_of(start + step * LANES, LANES), LANES), :]
            b = b.astype(f32)
            part[grad, here, :] = b
            return (
                sums[0] + jnp.sum(a * a, axis=0, keepdims=True),
                sums[1] + jnp.sum(b * b, axis=0, keepdims=True),
                sums[2] + jnp.sum(a * b, axis=0, keepdims=True),
            )

        sums = lax.fori_loop(0, size // LANES, body, (zero, zero, zero))
        return begin_totals(grad, level, *[whole(s) for s in sums])

    def finish(grad, coefs):
        size = half >> (levels - 1)
        target = (out_gate, out_up, out_down)[grad]

        @pl.loop(0, size // LANES)
        def _(step):
            here = pl.ds(pl.multiple_of(step * LANES, LANES), LANES)
            value = coefs[0] * own[grad, here, :] + coefs[1] * part[grad, here, :]
            if grad == 2:
                target[0, :, here] = value.T
            else:
                target[0, here, :] = value

    for copy in sca_to_mate + tok_to_mate:
        copy.wait_recv()
    act_to_mate[2].wait_recv()
    pending = {2: first_level(2)}

    @pl.loop(0, slots // ROWS)
    def _(step):
        rows = pl.ds(pl.multiple_of(step * ROWS, ROWS), ROWS)
        back = dot(acts[0, rows, :], wg[...], 1, 1) + dot(acts[1, rows, :], wu[...], 1, 1)
        ret_send[rows, 0:width] = back.astype(bf16)
        output = dot(acts[2, rows, :], wd[...])
        score = jnp.sum(output * cotp[rows, 0:width].astype(f32), axis=1, keepdims=True)
        ret_send[rows, width:] = jnp.broadcast_to(score, (ROWS, LANES)).astype(bf16)

    ret_copies = []
    for i in order:
        k = lax.rem(me + i, experts)
        copy = pltpu.make_async_remote_copy(
            ret_send.at[block(k)], ret_recv.at[block(me)], sr_sem.at[i], rr_sem.at[i],
            device_id={"expert": k}, device_id_type=MESH,
        )
        copy.start()
        ret_copies.append(copy)
    ret_recv[block(me), :] = ret_send[block(me), :]

    moving = {}
    for grad in (2, 1, 0):
        if grad != 2:
            act_to_mate[grad].wait_recv()
            pending[grad] = first_level(grad)
        coefs = end_totals(grad, 0, pending[grad])
        if levels > 1:
            moving[grad] = hand_over(grad, 1, coefs)
        else:
            finish(grad, coefs)
    for level in range(1, levels):
        for grad in (2, 1, 0):
            pending[grad] = next_level(grad, level, moving[grad])
            coefs = end_totals(grad, level, pending[grad])
            if level + 1 < levels:
                moving[grad] = hand_over(grad, level + 1, coefs)
            else:
                finish(grad, coefs)

    for copy in ret_copies:
        copy.wait_recv()

    @pl.loop(0, width // 512)
    def _(step):
        columns = pl.ds(pl.multiple_of(step * 512, 512), 512)
        out_in[:, columns] = dot(select[...], ret_recv[:, columns], 0, 0).astype(bf16)

    chosen_by = rout[...]
    scores = jnp.zeros((tokens, chosen_by.shape[1]), f32)
    for k in range(experts):
        rows = slice(k * capp, (k + 1) * capp)
        score = dot(select[rows, :], ret_recv[rows, width:], 0, 0)
        scores = scores + jnp.where(chosen_by == k, score[:, 0 : chosen_by.shape[1]], 0.0)
    out_router[...] = scores.astype(bf16)

    for copy in tok_copies + cot_copies + ret_copies + y_copies + tot_copies + x_copies:
        copy.wait_send()


def kernel(
    experts, replicas, cap, capp,
    tok, cot, rout, rout_t, prob_t, wg_hbm, wu_hbm, wd_hbm,
    out_gate, out_up, out_down, out_in, out_router,
    wg, wu, wd, ranks, weights, select, send_tok, send_cot, got_tok, got_cot, routed, cotp, scaled,
    gate_pre, up_pre, acts, p_routed, p_scaled, p_acts, ret_send, ret_recv,
    grads, gram_send, gram_recv,
    w_sem, st_sem, rt_sem, sc_sem, rc_sem, sr_sem, rr_sem,
    yts_sem, ytr_sem, yss_sem, ysr_sem, yas_sem, yar_sem, gs_sem, gr_sem, kts_sem, ktr_sem, kcs_sem, kcr_sem,
):
    me = lax.axis_index("expert")
    dp = lax.axis_index("dp")
    tokens, width = tok.shape
    hidden = wg.shape[1]
    slots = experts * capp
    levels = replicas.bit_length() - 1
    quarter = width // replicas
    bits = [lax.rem(dp // (1 << b), 2) for b in range(levels)]
    mates = [
        dp + sum((1 << b) * (1 - 2 * bits[b]) for b in range(levels) if j >> b & 1)
        for j in range(replicas)
    ]
    others = range(1, replicas)
    order = sorted(range(1, experts), key=lambda i: abs(2 * i - experts))
    chips = experts // 2
    here_chip, core = me // 2, lax.rem(me, 2)
    sibling = me + 1 - 2 * core
    both = -(-2 * cap // 16) * 16
    offset, shift = cap // 16 * 16, cap % 16
    chip_order = sorted(range(1, chips), key=lambda i: abs(2 * i - chips))

    def block(index):
        return pl.ds(pl.multiple_of(index * capp, capp), capp)

    loads = [
        pltpu.make_async_copy(src.at[0], dst, w_sem.at[j])
        for j, (src, dst) in enumerate(((wg_hbm, wg), (wu_hbm, wu), (wd_hbm, wd)))
    ]
    for load in loads:
        load.start()

    barrier = pltpu.get_barrier_semaphore()
    for i in range(1, experts):
        pl.semaphore_signal(
            barrier, inc=1, device_id={"expert": lax.rem(me + i, experts)}, device_id_type=MESH
        )
    for mate in mates[1:]:
        pl.semaphore_signal(barrier, inc=1, device_id={"dp": mate}, device_id_type=MESH)

    first, second = rout_t[0:1, :], rout_t[1:2, :]
    names = lax.broadcasted_iota(i32, ranks.shape, 0)
    is_first, is_second = names == first, names == second
    member = jnp.where(is_first | is_second, 1.0, 0.0).astype(f32)
    earlier = lax.broadcasted_iota(i32, (tokens, tokens), 0)
    later = lax.broadcasted_iota(i32, (tokens, tokens), 1)
    before = dot(member.astype(bf16), jnp.where(earlier < later, 1.0, 0.0).astype(bf16))
    ranks[...] = jnp.where(member > 0.0, before, -1024.0).astype(i32)
    weights[...] = jnp.where(
        is_first, prob_t[0:1, :], jnp.where(is_second, prob_t[1:2, :], 0.0)
    )
    slot = lax.broadcasted_iota(i32, (capp, tokens), 0)
    both_slot = lax.broadcasted_iota(i32, (both, tokens), 0)

    def pair(chip):
        return pl.ds(pl.multiple_of(chip * both, 16), both)

    def window(chip, which):
        return pl.ds(pl.multiple_of(chip * both + which * offset, 16), capp)

    def fill_tok(target, chip):
        low = both_slot == ranks[pl.ds(2 * chip, 1), :]
        high = both_slot == cap + ranks[pl.ds(2 * chip + 1, 1), :]
        chosen = jnp.where(low | high, 1.0, 0.0).astype(bf16)
        target[pair(chip), :] = dot(chosen, tok[...]).astype(bf16)

    def fill_cot(target, chip):
        low = both_slot == ranks[pl.ds(2 * chip, 1), :]
        high = both_slot == cap + ranks[pl.ds(2 * chip + 1, 1), :]
        chosen = jnp.where(low | high, 1.0, 0.0).astype(bf16)
        held = jnp.where(low, weights[pl.ds(2 * chip, 1), :], 0.0)
        held = jnp.where(high, weights[pl.ds(2 * chip + 1, 1), :], held)
        weight = jnp.sum(held, axis=1, keepdims=True)
        target[pair(chip), 0:width] = dot(chosen, cot[...]).astype(bf16)
        target[pair(chip), width:] = jnp.broadcast_to(weight, (both, LANES)).astype(bf16)

    pl.semaphore_wait(barrier, experts + replicas - 2)

    tok_copies, cot_copies = [], []
    def to_chip(i, source, target, send_sem, recv_sem):
        chip = lax.rem(here_chip + i, chips)
        copy = pltpu.make_async_remote_copy(
            source.at[pair(chip)], target.at[pair(here_chip)], send_sem.at[i], recv_sem.at[i],
            device_id={"expert": 2 * chip + core}, device_id_type=MESH,
        )
        copy.start()
        return copy

    for i in chip_order:
        fill_tok(send_tok, lax.rem(here_chip + i, chips))
        tok_copies.append(to_chip(i, send_tok, got_tok, st_sem, rt_sem))
    for i in chip_order:
        fill_cot(send_cot, lax.rem(here_chip + i, chips))
        cot_copies.append(to_chip(i, send_cot, got_cot, sc_sem, rc_sem))
    fill_tok(got_tok, here_chip)
    fill_cot(got_cot, here_chip)
    for k in range(experts):
        picked = slot == ranks[k : k + 1, :] + k % 2 * shift
        select[k * capp : (k + 1) * capp, :] = jnp.where(picked, 1.0, 0.0).astype(bf16)

    core_copies = []

    def to_sibling(chip, i, source, target, send_sem, recv_sem):
        copy = pltpu.make_async_remote_copy(
            source.at[window(chip, 1 - core)], target.at[block(2 * chip + core)],
            send_sem.at[i], recv_sem.at[i], device_id={"expert": sibling}, device_id_type=MESH,
        )
        copy.start()
        core_copies.append(copy)
        return copy

    y_copies = []

    def columns_of(mate):
        return pl.ds(pl.multiple_of(mate * quarter, LANES), quarter)

    def to_mate(j, source, target, send_sem, recv_sem):
        copy = pltpu.make_async_remote_copy(
            source, target, send_sem, recv_sem, device_id={"dp": mates[j]}, device_id_type=MESH
        )
        copy.start()
        y_copies.append(copy)
        return copy

    tok_to_mate, sca_to_mate, act_to_mate = [], [], {}
    def spread_tok(which, i):
        for j in others:
            tok_to_mate.append(to_mate(
                j, routed.at[block(which), columns_of(mates[j])], p_routed.at[j, block(which)],
                yts_sem.at[j, i], ytr_sem.at[j, i],
            ))

    def from_sibling(chip, i, copy):
        copy.wait_recv()
        spread_tok(2 * chip + 1 - core, 2 * i + 1)

    last = None
    for position, i in enumerate([0] + chip_order):
        chip = lax.rem(here_chip + chips - i, chips)
        if i:
            tok_copies[position - 1].wait_recv()
        copy = to_sibling(chip, i, got_tok, routed, kts_sem, ktr_sem)
        routed[block(2 * chip + core), :] = got_tok[window(chip, core), :]
        if last:
            from_sibling(*last)
        spread_tok(2 * chip + core, 2 * i)
        last = (chip, i, copy)
    from_sibling(*last)

    loads[0].wait()
    loads[1].wait()

    @pl.loop(0, slots // ROWS)
    def _(step):
        rows = pl.ds(pl.multiple_of(step * ROWS, ROWS), ROWS)
        x = routed[rows, :]
        g = dot(x, wg[...])
        u = dot(x, wu[...])
        gate_pre[rows, :] = g
        up_pre[rows, :] = u
        acts[2, rows, :] = (g * jax.nn.sigmoid(g) * u).astype(bf16)

    def send_act(grad, j, source=None):
        act_to_mate[grad, source or j] = to_mate(
            j, p_acts.at[grad, source ^ j] if source else acts.at[grad],
            p_acts.at[grad, source or j],
            yas_sem.at[grad, source or j], yar_sem.at[grad, source or j],
        )

    for j in others:
        send_act(2, j)

    line = lax.broadcasted_iota(i32, (capp, 1), 0)
    valid = (line >= core * shift) & (line < core * shift + cap)

    def spread_cot(which, i):
        weight = jnp.where(valid, cotp[block(which), width:].astype(f32)[:, 0:1], 0.0)
        scaled[block(which), :] = (
            weight * cotp[block(which), 0:width].astype(f32)
        ).astype(bf16)
        for j in others:
            sca_to_mate.append(to_mate(
                j, scaled.at[block(which), columns_of(mates[j])], p_scaled.at[j, block(which)],
                yss_sem.at[j, i], ysr_sem.at[j, i],
            ))

    def cot_from_sibling(chip, i, copy):
        copy.wait_recv()
        spread_cot(2 * chip + 1 - core, 2 * i + 1)

    last = None
    for position, i in enumerate([0] + chip_order):
        chip = lax.rem(here_chip + chips - i, chips)
        if i:
            cot_copies[position - 1].wait_recv()
        copy = to_sibling(chip, i, got_cot, cotp, kcs_sem, kcr_sem)
        cotp[block(2 * chip + core), :] = got_cot[window(chip, core), :]
        if last:
            cot_from_sibling(*last)
        spread_cot(2 * chip + core, 2 * i)
        last = (chip, i, copy)
    cot_from_sibling(*last)

    loads[2].wait()

    @pl.loop(0, slots // ROWS)
    def _(step):
        rows = pl.ds(pl.multiple_of(step * ROWS, ROWS), ROWS)
        hg = dot(scaled[rows, :], wd[...], 1, 1)
        g, u = gate_pre[rows, :], up_pre[rows, :]
        s = jax.nn.sigmoid(g)
        acts[1, rows, :] = (hg * (g * s)).astype(bf16)
        acts[0, rows, :] = (hg * u * s * (1.0 + g * (1.0 - s))).astype(bf16)

    relayed = replicas == 4
    near = (1, 2) if relayed else others
    for grad in (1, 0):
        for j in near:
            send_act(grad, j)

    scaling = 1.0 / (experts * cap)
    pairs = [(i, j) for i in range(replicas) for j in range(i, replicas)]

    def grad_of(grad, j):
        left, p_left = (scaled, p_scaled) if grad == 2 else (routed, p_routed)

        @pl.loop(0, quarter // LANES)
        def _(step):
            here = pl.ds(pl.multiple_of(step * LANES, LANES), LANES)
            if j:
                x, y = p_left[j, :, here], p_acts[grad, j]
            else:
                there = pl.multiple_of(dp * quarter + step * LANES, LANES)
                x, y = left[:, pl.ds(there, LANES)], acts[grad]
            grads[grad, j, here, :] = dot(x, y, 0, 0) * scaling

    def gram_of(grad):
        def body(step, sums):
            here = pl.ds(pl.multiple_of(step * 8, 8), 8)
            held = [grads[grad, j, here, :] for j in range(replicas)]
            return tuple(s + held[i] * held[j] for s, (i, j) in zip(sums, pairs))

        zero = jnp.zeros((8, hidden), f32)
        sums = lax.fori_loop(0, quarter // 8, body, (zero,) * len(pairs))
        for row, total in enumerate(sums):
            total = jnp.sum(jnp.sum(total, axis=0, keepdims=True), axis=1, keepdims=True)
            gram_send[grad, row : row + 1, :] = jnp.broadcast_to(total, (1, LANES))

    def combine(grad):
        def entry(i, j):
            total = 0.0
            for m in range(replicas):
                row = pairs.index(tuple(sorted((i ^ m, j ^ m))))
                held = gram_recv[m, grad, row : row + 1, :] if m else gram_send[grad, row : row + 1, :]
                total = total + held
            return total

        gram = {pair: entry(*pair) for pair in pairs}

        def product(left, right):
            return sum(
                left[i] * right[j] * gram[min(i, j), max(i, j)] for i in left for j in right
            )

        vectors = [{j: jnp.ones((1, LANES), f32)} for j in range(replicas)]
        while len(vectors) > 1:
            count = len(vectors) // 2
            joined = []
            for j in range(count):
                a, b = vectors[j], vectors[j + count]
                inner = product(a, b)
                na = jnp.maximum(product(a, a), 0.0)
                nb = jnp.maximum(product(b, b), 0.0)
                ca = 1.0 - inner / (2.0 * (na + epsilon))
                cb = 1.0 - inner / (2.0 * (nb + epsilon))
                joined.append({
                    **{i: ca * c for i, c in a.items()}, **{i: cb * c for i, c in b.items()}
                })
            vectors = joined
        coefs = [vectors[0][j][:, 0:1] for j in range(replicas)]
        target = (out_gate, out_up, out_down)[grad]

        @pl.loop(0, quarter // LANES)
        def _(step):
            here = pl.ds(pl.multiple_of(step * LANES, LANES), LANES)
            value = coefs[0] * grads[grad, 0, here, :]
            for j in others:
                value = value + coefs[j] * grads[grad, j, here, :]
            if grad == 2:
                target[0, :, here] = value.T
            else:
                target[0, here, :] = value

    @pl.loop(0, slots // ROWS)
    def _(step):
        rows = pl.ds(pl.multiple_of(step * ROWS, ROWS), ROWS)
        back = dot(acts[0, rows, :], wg[...], 1, 1) + dot(acts[1, rows, :], wu[...], 1, 1)
        ret_send[rows, 0:width] = back.astype(bf16)
        output = dot(acts[2, rows, :], wd[...])
        score = jnp.sum(output * cotp[rows, 0:width].astype(f32), axis=1, keepdims=True)
        ret_send[rows, width:] = jnp.broadcast_to(score, (ROWS, LANES)).astype(bf16)

    ret_copies = []
    for i in order:
        k = lax.rem(me + i, experts)
        copy = pltpu.make_async_remote_copy(
            ret_send.at[block(k)], ret_recv.at[block(me)], sr_sem.at[i], rr_sem.at[i],
            device_id={"expert": k}, device_id_type=MESH,
        )
        copy.start()
        ret_copies.append(copy)
    ret_recv[block(me), :] = ret_send[block(me), :]

    for copy in sca_to_mate + tok_to_mate:
        copy.wait_recv()
    for grad in (2, 1, 0):
        grad_of(grad, 0)
    for j in others:
        act_to_mate[2, j].wait_recv()
        grad_of(2, j)
    gram_of(2)
    for grad, far in ((1, 1), (0, 2)):
        for j in near:
            act_to_mate[grad, j].wait_recv()
        if relayed:
            send_act(grad, far, 3)
        for j in near:
            grad_of(grad, j)
    for grad in (1, 0):
        if relayed:
            act_to_mate[grad, 3].wait_recv()
            grad_of(grad, 3)
        gram_of(grad)
    gram_copies = []
    for j in others:
        copy = pltpu.make_async_remote_copy(
            gram_send, gram_recv.at[j], gs_sem.at[j], gr_sem.at[j],
            device_id={"dp": mates[j]}, device_id_type=MESH,
        )
        copy.start()
        gram_copies.append(copy)
    for copy in ret_copies:
        copy.wait_recv()

    @pl.loop(0, width // 512)
    def _(step):
        columns = pl.ds(pl.multiple_of(step * 512, 512), 512)
        out_in[:, columns] = dot(select[...], ret_recv[:, columns], 0, 0).astype(bf16)

    chosen_by = rout[...]
    scores = jnp.zeros((tokens, chosen_by.shape[1]), f32)
    for k in range(experts):
        rows = slice(k * capp, (k + 1) * capp)
        score = dot(select[rows, :], ret_recv[rows, width:], 0, 0)
        scores = scores + jnp.where(chosen_by == k, score[:, 0 : chosen_by.shape[1]], 0.0)
    out_router[...] = scores.astype(bf16)

    for copy in gram_copies:
        copy.wait_recv()
    for grad in (2, 1, 0):
        combine(grad)

    for copy in tok_copies + cot_copies + ret_copies + y_copies + gram_copies + core_copies:
        copy.wait_send()


def per_device(experts, replicas, tokens, routing, probs, cotangent, w_gate, w_up, w_down):
    rows, top = routing.shape
    width = tokens.shape[1]
    hidden = w_gate.shape[2]
    cap = 5 * rows * top // (4 * experts)
    capp = -(-cap // 16) * 16
    slots = experts * capp
    levels = replicas.bit_length() - 1
    half = width // 2
    shard = width // replicas
    direct = replicas <= 4
    steps = 3 * (levels * (levels + 1) // 2)
    wide = width + LANES
    vm, dma = pltpu.VMEM, pltpu.SemaphoreType.DMA
    in_vmem = pl.BlockSpec(memory_space=pltpu.VMEM)
    in_any = pl.BlockSpec(memory_space=pl.ANY)
    paired = experts // 2 * (-(-2 * cap // 16) * 16)
    names = max(16, experts)
    grams = -(-replicas * (replicas + 1) // 16) * 8
    return tuple(pl.pallas_call(
        functools.partial(kernel if direct else halving_kernel, experts, replicas, cap, capp),
        out_shape=(
            jax.ShapeDtypeStruct((1, shard, hidden), f32),
            jax.ShapeDtypeStruct((1, shard, hidden), f32),
            jax.ShapeDtypeStruct((1, hidden, shard), f32),
            jax.ShapeDtypeStruct((rows, width), bf16),
            jax.ShapeDtypeStruct((rows, top), bf16),
        ),
        in_specs=[in_vmem] * 5 + [in_any] * 3,
        out_specs=(in_vmem,) * 5,
        scratch_shapes=[
            vm((width, hidden), bf16), vm((width, hidden), bf16), vm((hidden, width), bf16),
            vm((names, rows), i32), vm((names, rows), f32), vm((slots, rows), bf16),
        ] + ([
            vm((paired, width), bf16), vm((paired, wide), bf16),
            vm((paired, width), bf16), vm((paired, wide), bf16),
        ] if direct else [
            vm((slots, width), bf16), vm((slots, wide), bf16),
        ]) + [
            vm((slots, width), bf16), vm((slots, wide), bf16), vm((slots, width), bf16),
            vm((slots, hidden), f32), vm((slots, hidden), f32), vm((3, slots, hidden), bf16),
        ] + ([
            vm((replicas, slots, shard), bf16), vm((replicas, slots, shard), bf16),
            vm((3, replicas, slots, hidden), bf16),
        ] if direct else [
            vm((slots, half), bf16), vm((slots, half), bf16), vm((3, slots, hidden), bf16),
        ]) + [
            vm((slots, wide), bf16), vm((slots, wide), bf16),
        ] + ([
            vm((3, replicas, shard, hidden), f32),
            vm((3, grams, LANES), f32), vm((replicas, 3, grams, LANES), f32),
        ] if direct else [
            vm((3, half, hidden), f32), vm((3, half, hidden), f32),
            vm((3, half, hidden), bf16), vm((3, half, hidden), bf16),
            vm((steps, 8, LANES), f32), vm((steps, 8, LANES), f32),
        ]) + [dma((3,))] + [dma((experts,))] * 6 + ([
            dma((replicas, experts)), dma((replicas, experts)),
            dma((replicas, experts)), dma((replicas, experts)),
            dma((3, replicas)), dma((3, replicas)), dma((replicas,)), dma((replicas,)),
            dma((experts // 2,)), dma((experts // 2,)), dma((experts // 2,)), dma((experts // 2,)),
        ] if direct else [dma((experts,))] * 4 + [dma((3,))] * 2
            + [dma((3 * max(levels - 1, 1),))] * 2 + [dma((steps,))] * 2),
        compiler_params=pltpu.CompilerParams(
            collective_id=0, has_side_effects=True, vmem_limit_bytes=67_000_000
        ),
        name="adasum_moe",
    )(
        tokens, cotangent, routing, routing.T, probs.T.astype(f32), w_gate, w_up, w_down
    ))


def solution(mesh):
    rows = P(("dp", "expert"), None)
    return jax.shard_map(
        functools.partial(per_device, mesh.shape["expert"], mesh.shape["dp"]),
        mesh=mesh,
        in_specs=(rows,) * 4 + (P("expert", None, None),) * 3,
        out_specs=(
            P("expert", "dp", None),
            P("expert", "dp", None),
            P("expert", None, "dp"),
            rows,
            rows,
        ),
        check_vma=False,
    )
```
